32 devices in a mesh: seq: 8 (over y, x, core), mdl: 4 (over z).
Axes of the slice: x: 2, y: 2, z: 4, core: 2. Of those that a mesh axis runs over, the one named last changes fastest.
Arguments:
- layer_in: float32 [4, 2, 1024, 2048], P(None, None, ('seq', 'mdl')), may hold values from -6 to 6
- doc_ids: int32 [4, 2, 1024], replicated, may hold values from -1 to 20, as said below
- cotangent: float32 [4, 2, 1024, 2048], P(None, None, ('seq', 'mdl')), may hold values from -6 to 6
- norm_params: float32 [4, 2048], replicated
- w_qkv: float32 [2048, 3, 2048], P('seq', None, 'mdl'), may hold values from -0.125 to 0.125
- w_out: float32 [2048, 2048], P('seq', 'mdl'), may hold values from -0.375 to 0.375
- w_up: float32 [2048, 8192], P('seq', 'mdl'), may hold values from -0.125 to 0.125
- w_down: float32 [2048, 8192], P('seq', 'mdl'), may hold values from -0.0625 to 0.0625
- norm_moment: float32 [4, 2048], replicated, may hold values from -543.058 to 543.058
- norm_average: float32 [4, 2048], replicated, may hold values from 0.5 to 1.5
- qkv_moment: float32 [2048, 3, 2048], P('seq', None, 'mdl'), may hold values from -452.54834 to 452.54834
- qkv_average: float32 [2048, 3, 2048], P('seq', None, 'mdl'), may hold values from -0.125 to 0.125
- out_moment: float32 [2048, 2048], P('seq', 'mdl'), may hold values from -452.54834 to 452.54834
- out_average: float32 [2048, 2048], P('seq', 'mdl'), may hold values from -0.375 to 0.375
- up_moment: float32 [2048, 8192], P('seq', 'mdl'), may hold values from -452.54834 to 452.54834
- up_average: float32 [2048, 8192], P('seq', 'mdl'), may hold values from -0.125 to 0.125
- down_moment: float32 [2048, 8192], P('seq', 'mdl'), may hold values from -452.54834 to 452.54834
- down_average: float32 [2048, 8192], P('seq', 'mdl'), may hold values from -0.0625 to 0.0625
Outputs:
- layer_out: float32 [4, 2, 1024, 2048], P(None, None, ('seq', 'mdl'))
- input_grad: float32 [4, 2, 1024, 2048], P(None, None, ('seq', 'mdl'))
- norm_moment_new: float32 [4, 2048], replicated
- norm_average_new: float32 [4, 2048], replicated
- norm_params_new: float32 [4, 2048], replicated
- norm_params_half: bfloat16 [4, 2048], replicated
- qkv_moment_new: float32 [2048, 3, 2048], P('seq', None, 'mdl')
- qkv_average_new: float32 [2048, 3, 2048], P('seq', None, 'mdl')
- qkv_weight_new: float32 [2048, 3, 2048], P('seq', None, 'mdl')
- qkv_weight_half: bfloat16 [2048, 3, 2048], P('seq', None, 'mdl')
- out_moment_new: float32 [2048, 2048], P('seq', 'mdl')
- out_average_new: float32 [2048, 2048], P('seq', 'mdl')
- out_weight_new: float32 [2048, 2048], P('seq', 'mdl')
- out_weight_half: bfloat16 [2048, 2048], P('seq', 'mdl')
- up_moment_new: float32 [2048, 8192], P('seq', 'mdl')
- up_average_new: float32 [2048, 8192], P('seq', 'mdl')
- up_weight_new: float32 [2048, 8192], P('seq', 'mdl')
- up_weight_half: bfloat16 [2048, 8192], P('seq', 'mdl')
- down_moment_new: float32 [2048, 8192], P('seq', 'mdl')
- down_average_new: float32 [2048, 8192], P('seq', 'mdl')
- down_weight_new: float32 [2048, 8192], P('seq', 'mdl')
- down_weight_half: bfloat16 [2048, 8192], P('seq', 'mdl')
The draws below stay inside these ranges and needn't reach their ends.
Inputs may be any that keep to these rules, and one draw needn't show every extreme that they name: `doc_ids`: documents are numbered from 0 and never fall along a row; each row ends in 1 to 128 padding slots marked -1; every document of a row but the last holds 51 to 1024 slots, and the last may be cut short by the row's padding; some row holds one document over all its slots but its padding.
All inputs are finite; a program needn't handle non-finite values.
Results may differ from the reference program's by a relative error of at most 0.015.
Values may be sent and summed in bfloat16 or wider, within the bound.
No kernel may reach another device: no remote copies, remote signals or barrier semaphores. Data moves between devices by JAX's collectives and lax.ppermute only.
A program may use at most 320 MiB of HBM per device.

```python
import jax
import jax.numpy as jnp
from jax import lax

D = 2048
HEADS = 32
HD = 64
FF = 8192
SLOT_DEV = 128
ROWS = 2
MB = 4
SLOTS = 1024
TOKENS = 8192


def draw_doc_ids(key, part):
    pieces = MB * ROWS
    first_key = jax.random.fold_in(key, 11)
    second_key = jax.random.fold_in(key, 12)
    third_key = jax.random.fold_in(key, 13)
    fourth_key = jax.random.fold_in(key, 14)
    divisors = jax.random.randint(first_key, (pieces, 24), 1, 21)
    piece_index = jnp.arange(pieces, dtype=jnp.int32)[:, None]
    long_piece = jax.random.randint(third_key, (), 0, pieces).astype(jnp.int32)
    short_piece = (long_piece + 1) % pieces
    divisors = jnp.where(piece_index == short_piece, 20, divisors)
    divisors = jnp.where(piece_index == long_piece, 1, divisors)
    lengths = SLOTS // divisors
    ends = jnp.cumsum(lengths, axis=1)
    positions = jnp.arange(SLOTS, dtype=jnp.int32)
    numbers = jnp.sum((ends[:, None, :] <= positions[None, :, None]).astype(jnp.int32), axis=2)
    padding = jax.random.randint(second_key, (pieces, 1), 1, SLOTS // 8 + 1)
    long_padding = jax.random.randint(fourth_key, (pieces, 1), 1, max(SLOT_DEV // 2, 1) + 1)
    padding = jnp.where(piece_index == short_piece, 1, padding)
    padding = jnp.where(piece_index == long_piece, long_padding, padding)
    numbers = jnp.where(positions[None, :] >= SLOTS - padding, -1, numbers)
    return numbers.reshape(MB, ROWS, SLOTS).astype(jnp.int32)


def draw_norm_params(key, part):
    noise = jax.random.normal(jax.random.fold_in(key, 21), (4, D), jnp.float32)
    scales = jnp.array([0.15, 0.3, 0.15, 0.3], jnp.float32)[:, None]
    shifts = jnp.array([1.0, 0.0, 1.0, 0.0], jnp.float32)[:, None]
    return shifts + scales * noise


def shard_levels(key, shape, cuts, smallest, high):
    level, own = 1.0, jax.random.fold_in(key, 6)
    for dim, blocks in cuts:
        steps = jnp.exp(jax.random.uniform(jax.random.fold_in(own, dim), (blocks,), jnp.float32, smallest / len(cuts), high / len(cuts)))
        level = level * jnp.repeat(steps, shape[dim] // blocks).reshape([-1 if axis == dim else 1 for axis in range(len(shape))])
    return level


def gaussian(rng, shape, width, limit, cuts=(), kind=jnp.bfloat16):
    values = width * jax.random.normal(rng, shape, jnp.float32)
    if cuts:
        values = values * shard_levels(rng, shape, cuts, -0.22, 0.18)
    return jnp.clip(values, -limit, limit).astype(kind)


def setup_inputs(seed: int = 0) -> dict:
    splits = jax.random.split(jax.random.key(seed), 19)
    return {
        "layer_in": gaussian(splits[0], (MB, ROWS, SLOTS, D), 1.0, 6.0, ((2, 32),), jnp.float32),
        "doc_ids": draw_doc_ids(jax.random.fold_in(splits[18], 71), 0),
        "cotangent": gaussian(splits[2], (MB, ROWS, SLOTS, D), 1.0, 6.0, ((2, 32),), jnp.float32),
        "norm_params": draw_norm_params(jax.random.fold_in(splits[18], 71), 0),
        "w_qkv": gaussian(splits[4], (D, 3, D), D ** -0.5, 0.125, ((0, 8), (2, 4)), jnp.float32),
        "w_out": gaussian(splits[5], (D, D), (D // 8) ** -0.5, 0.375, ((0, 8), (1, 4)), jnp.float32),
        "w_up": gaussian(splits[6], (D, FF), D ** -0.5, 0.125, ((0, 8), (1, 4)), jnp.float32),
        "w_down": gaussian(splits[7], (D, FF), FF ** -0.5, 0.0625, ((0, 8), (1, 4)), jnp.float32),
        "norm_moment": gaussian(splits[8], (4, D), (0.5 * TOKENS ** 0.5), 543.058, (), jnp.float32),
        "norm_average": jnp.clip(1.0 + 0.1 * jax.random.normal(splits[9], (4, D), jnp.float32), 0.5, 1.5),
        "qkv_moment": gaussian(splits[10], (D, 3, D), (0.4 * TOKENS ** 0.5), 452.54834, ((0, 8), (2, 4)), jnp.float32),
        "qkv_average": gaussian(splits[11], (D, 3, D), D ** -0.5, 0.125, ((0, 8), (2, 4)), jnp.float32),
        "out_moment": gaussian(splits[12], (D, D), (0.4 * TOKENS ** 0.5), 452.54834, ((0, 8), (1, 4)), jnp.float32),
        "out_average": gaussian(splits[13], (D, D), (D // 8) ** -0.5, 0.375, ((0, 8), (1, 4)), jnp.float32),
        "up_moment": gaussian(splits[14], (D, FF), (0.4 * TOKENS ** 0.5), 452.54834, ((0, 8), (1, 4)), jnp.float32),
        "up_average": gaussian(splits[15], (D, FF), D ** -0.5, 0.125, ((0, 8), (1, 4)), jnp.float32),
        "down_moment": gaussian(splits[16], (D, FF), (0.4 * TOKENS ** 0.5), 452.54834, ((0, 8), (1, 4)), jnp.float32),
        "down_average": gaussian(splits[17], (D, FF), FF ** -0.5, 0.0625, ((0, 8), (1, 4)), jnp.float32),
    }


@jax.custom_vjp
def low(v):
    return lax.optimization_barrier(v.astype(jnp.bfloat16)).astype(jnp.float32)

@jax.custom_vjp
def low_back(v):
    return v

def low_keep(v):
    return (low(v), None)

def low_pass(kept, grad):
    return (grad,)

def back_keep(v):
    return (v, None)

def back_low(kept, grad):
    return (low(grad),)
low.defvjp(low_keep, low_pass)
low_back.defvjp(back_keep, back_low)
HIGHEST = lax.Precision.HIGHEST
HALF_ROOT = 0.7071067811865476

def layer_norm(values, gain, shift):
    row_mean = lax.optimization_barrier(jnp.mean(values, -1, keepdims=True))
    centred = values - row_mean
    spread = lax.optimization_barrier(jnp.mean(centred * centred, -1, keepdims=True))
    return centred * lax.rsqrt(spread + 1e-05) * gain + shift

def gelu_exact(inputs):
    return 0.5 * inputs * (1.0 + lax.erf(inputs * HALF_ROOT))

def row_attend(queries, keys_all, values_all, doc_row):
    positions = jnp.arange(SLOTS, dtype=jnp.int32)
    allowed = (doc_row[:, None] == doc_row[None, :]) & (doc_row[:, None] >= 0) & (positions[None, :] <= positions[:, None]) | (positions[None, :] == positions[:, None])

    def one_head(parts):
        query_head, key_head, value_head = parts
        scores = low_back(jnp.dot(query_head, key_head.T, precision=HIGHEST) * HD ** (-0.5))
        masked = jnp.where(allowed, scores, -1e+30)
        row_max = lax.optimization_barrier(jnp.max(masked, -1, keepdims=True))
        expos = jnp.exp(masked - row_max)
        probs = expos / lax.optimization_barrier(jnp.sum(expos, -1, keepdims=True))
        return jnp.dot(low(probs), value_head, precision=HIGHEST)
    heads_out = lax.map(jax.checkpoint(one_head), (queries.transpose(1, 0, 2), keys_all.transpose(1, 0, 2), values_all.transpose(1, 0, 2)))
    return heads_out.transpose(1, 0, 2)

def block(inputs, doc_rows, normp, weight_qkv, weight_out, weight_up, weight_down):
    norm_one = low(layer_norm(inputs, normp[0], normp[1]))
    projected = low(low_back(jnp.einsum('rsd,dct->rsct', norm_one, weight_qkv, precision=HIGHEST)))
    split = projected.reshape(ROWS, SLOTS, 3, HEADS, HD)
    attended = lax.map(lambda parts: row_attend(parts[0], parts[1], parts[2], parts[3]), (split[:, :, 0], split[:, :, 1], split[:, :, 2], doc_rows))
    attended = low(low_back(attended.reshape(ROWS, SLOTS, D)))
    middle = inputs + low_back(jnp.einsum('rse,de->rsd', attended, weight_out, precision=HIGHEST))
    norm_two = low(layer_norm(middle, normp[2], normp[3]))
    up_proj = low_back(jnp.einsum('rsd,df->rsf', norm_two, weight_up, precision=HIGHEST))
    hidden = low(gelu_exact(up_proj))
    return middle + low_back(jnp.einsum('rsf,df->rsd', hidden, weight_down, precision=HIGHEST))

def update_param(weight, grad, moment, average, rate):
    new_moment = 0.5 * moment + grad
    new_weight = weight - rate * (grad + 0.5 * new_moment)
    new_average = 0.5 * average + 0.5 * new_weight
    return (new_moment, new_average, new_weight, new_weight.astype(jnp.bfloat16))

def reference(layer_in, doc_ids, cotangent, norm_params, w_qkv, w_out, w_up, w_down, norm_moment, norm_average, qkv_moment, qkv_average, out_moment, out_average, up_moment, up_average, down_moment, down_average):

    def whole(inputs, normp, weight_qkv, weight_out, weight_up, weight_down):
        low_qkv = low(weight_qkv)
        low_out = low(weight_out)
        low_up = low(weight_up)
        low_down = low(weight_down)

        def scan_step(carry, items):
            return (carry, block(items[0], items[1], normp, low_qkv, low_out, low_up, low_down))
        unused, results = lax.scan(jax.checkpoint(scan_step), jnp.zeros((), jnp.float32), (inputs, doc_ids))
        return results
    layer_out, pullback = jax.vjp(whole, layer_in, norm_params, w_qkv, w_out, w_up, w_down)
    grads = pullback(cotangent)
    weight_rate = 0.02 * TOKENS ** (-0.5)
    norm_rate = 0.15 * TOKENS ** (-0.5)
    norm_new = update_param(norm_params, grads[1], norm_moment, norm_average, norm_rate)
    qkv_new = update_param(w_qkv, grads[2], qkv_moment, qkv_average, weight_rate)
    out_new = update_param(w_out, grads[3], out_moment, out_average, weight_rate)
    up_new = update_param(w_up, grads[4], up_moment, up_average, weight_rate)
    down_new = update_param(w_down, grads[5], down_moment, down_average, weight_rate)
    return (layer_out, grads[0], norm_new[0], norm_new[1], norm_new[2], norm_new[3], qkv_new[0], qkv_new[1], qkv_new[2], qkv_new[3], out_new[0], out_new[1], out_new[2], out_new[3], up_new[0], up_new[1], up_new[2], up_new[3], down_new[0], down_new[1], down_new[2], down_new[3])
```

```python
import functools

import jax
import jax.numpy as jnp
from jax import lax
from jax.experimental import pallas as pl
from jax.experimental.pallas import tpu as pltpu
from jax.sharding import PartitionSpec as P

HD = 64
LANES = 128
CHUNKS = 2

EPSILON = 1e-05
HALF_ROOT = 0.7071067811865476
INV_ROOT_TWO_PI = 0.3989422804014327
BF16 = jnp.bfloat16
F32 = jnp.float32


def norm_forward(values, gain, shift):
    row_mean = jnp.mean(values, -1, keepdims=True)
    centred = values - row_mean
    inv_std = lax.rsqrt(jnp.mean(centred * centred, -1, keepdims=True) + EPSILON)
    normed = centred * inv_std
    return (normed * gain + shift, normed, inv_std)


def norm_backward(upstream, normed, inv_std, gain):
    scaled = upstream * gain
    return inv_std * (
        scaled
        - jnp.mean(scaled, -1, keepdims=True)
        - normed * jnp.mean(scaled * normed, -1, keepdims=True)
    )


def update_param(weight, grad, moment, average, rate):
    new_moment = 0.5 * moment + grad
    new_weight = weight - rate * (grad + 0.5 * new_moment)
    new_average = 0.5 * average + 0.5 * new_weight
    return (new_moment, new_average, new_weight, new_weight.astype(BF16))


def dot(a, b, dims):
    return lax.dot_general(a, b, (dims, ((), ())), preferred_element_type=F32)


def ring_gather(block, axis):
    count = lax.axis_size(axis)
    pairs = [(i, (i + 1) % count) for i in range(count)]
    parts = [block]
    for _ in range(count - 1):
        parts.append(lax.ppermute(parts[-1], axis, pairs))
    return jnp.stack(parts)


def ring_scatter(parts, axis):
    count = lax.axis_size(axis)
    pairs = [(i, (i + 1) % count) for i in range(count)]
    carried = None
    for j in range(1, count):
        term = parts[j]
        if carried is not None:
            term = term + carried.astype(F32)
        carried = lax.ppermute(term.astype(BF16), axis, pairs)
    return parts[0] + carried.astype(F32)


def score_blocks(keys, queries, kpos, first, last, start, size):
    diag = dot(keys[start : start + size], queries, ((1,), (1,)))
    pos = kpos[start : start + size]
    diag = jnp.where((pos >= first) & (pos <= last), diag, -1e30)
    if not start:
        return [diag]
    ahead = dot(keys[:start], queries, ((1,), (1,)))
    return [jnp.where(kpos[:start] >= first, ahead, -1e30), diag]


def attend_kernel(kpos_ref, meta_ref, q_ref, k_ref, v_ref, o_ref, lse_ref, *, size, factor):
    slots = kpos_ref.shape[0]
    per = q_ref.shape[1] * q_ref.shape[2]
    heads = LANES // HD
    keys = k_ref[...].reshape(slots, LANES)
    values = v_ref[...].reshape(slots, LANES)
    kpos = kpos_ref[...]
    for start in range(0, slots, size):
        span = pl.ds(start // per, size // per)
        queries = q_ref[span].reshape(size, LANES) * factor
        first = meta_ref[0:1, start : start + size]
        last = meta_ref[1:2, start : start + size]
        outs = []
        for head in range(heads):
            cols = slice(head * HD, (head + 1) * HD)
            blocks = score_blocks(keys[:, cols], queries[:, cols], kpos, first, last, start, size)
            top = functools.reduce(jnp.maximum, [jnp.max(b, 0, keepdims=True) for b in blocks])
            blocks = [jnp.exp(b - top) for b in blocks]
            total = functools.reduce(jnp.add, [jnp.sum(b, 0, keepdims=True) for b in blocks])
            lse_ref[head : head + 1, start : start + size] = top + jnp.log(total)
            inverse = 1.0 / total
            out = None
            offset = 0
            for b in blocks:
                rows = slice(offset, offset + b.shape[0])
                offset += b.shape[0]
                term = dot(values[rows, cols], (b * inverse).astype(BF16), ((0,), (0,)))
                out = term if out is None else out + term
            outs.append(out)
        merged = jnp.concatenate(outs, 0).T.astype(BF16)
        o_ref[span] = merged.reshape(size // per, *o_ref.shape[1:])


def attend_back_kernel(
    kpos_ref, meta_ref, lse_ref, q_ref, k_ref, v_ref, g_ref, out_ref, dk_acc, dv_acc, *, size, factor
):
    slots = kpos_ref.shape[0]
    per = q_ref.shape[1] * q_ref.shape[2]
    heads = LANES // HD
    keys = k_ref[...].reshape(slots, LANES)
    values = v_ref[...].reshape(slots, LANES)
    kpos = kpos_ref[...]
    dk_acc[...] = jnp.zeros_like(dk_acc)
    dv_acc[...] = jnp.zeros_like(dv_acc)
    for start in range(0, slots, size):
        span = pl.ds(start // per, size // per)
        queries = q_ref[span].reshape(size, LANES) * factor
        upstream = g_ref[span].reshape(size, LANES)
        first = meta_ref[0:1, start : start + size]
        last = meta_ref[1:2, start : start + size]
        dqs, dks, dvs = [], [], []
        for head in range(heads):
            cols = slice(head * HD, (head + 1) * HD)
            blocks = score_blocks(keys[:, cols], queries[:, cols], kpos, first, last, start, size)
            lse = lse_ref[head : head + 1, start : start + size]
            probs = [jnp.exp(b - lse) for b in blocks]
            edges = [0] + ([start] if start else []) + [start + size]
            rows = [slice(a, b) for a, b in zip(edges[:-1], edges[1:])]
            back = [dot(values[r, cols], upstream[:, cols], ((1,), (1,))) for r in rows]
            terms = [p * b for p, b in zip(probs, back)]
            weighted = functools.reduce(jnp.add, [jnp.sum(t, 0, keepdims=True) for t in terms])
            score_back = [(t - p * weighted).astype(BF16) for t, p in zip(terms, probs)]
            dks.append([dot(s, queries[:, cols], ((1,), (0,))) for s in score_back])
            dvs.append([dot(p.astype(BF16), upstream[:, cols], ((1,), (0,))) for p in probs])
            dq = [dot(keys[r, cols], s, ((0,), (0,))) for r, s in zip(rows, score_back)]
            dqs.append(functools.reduce(jnp.add, dq) * factor)
        merged = jnp.concatenate(dqs, 0).T.astype(BF16)
        out_ref[span, 0] = merged.reshape(size // per, *out_ref.shape[2:])
        for i, r in enumerate(rows):
            dk_acc[r] += jnp.concatenate([d[i] for d in dks], 1)
            dv_acc[r] += jnp.concatenate([d[i] for d in dvs], 1)
    shape = (out_ref.shape[0], *out_ref.shape[2:])
    out_ref[:, 1] = dk_acc[...].astype(BF16).reshape(shape)
    out_ref[:, 2] = dv_acc[...].astype(BF16).reshape(shape)


def kind_spec(shape, kind):
    seq, _, _, blocks, short, lanes = shape
    return pl.BlockSpec(
        (seq, None, None, blocks, short, lanes), lambda r, kind=kind: (0, kind, r, 0, 0, 0)
    )


def attention(qkv, kpos, meta, size):
    seq, _, units, blocks, short, lanes = qkv.shape
    slots = kpos.shape[0]
    heads = LANES // HD
    work = units * heads * slots * slots * 5 // 8
    return pl.pallas_call(
        functools.partial(attend_kernel, size=size, factor=HD**-0.5),
        grid=(units,),
        in_specs=[
            pl.BlockSpec((slots, 1), lambda r: (0, 0)),
            pl.BlockSpec((None, 2, slots), lambda r: (r, 0, 0)),
            *(kind_spec(qkv.shape, kind) for kind in range(3)),
        ],
        out_specs=[
            pl.BlockSpec((seq, None, blocks, short, lanes), lambda r: (0, r, 0, 0, 0)),
            pl.BlockSpec((None, heads, slots), lambda r: (r, 0, 0)),
        ],
        out_shape=[
            jax.ShapeDtypeStruct((seq, units, blocks, short, lanes), BF16),
            jax.ShapeDtypeStruct((units, heads, slots), F32),
        ],
        compiler_params=pltpu.CompilerParams(vmem_limit_bytes=48 << 20),
        cost_estimate=pl.CostEstimate(
            flops=work * HD * 4 * 4, bytes_accessed=units * slots * LANES * 8, transcendentals=work
        ),
        name="attend",
    )(kpos, meta, qkv, qkv, qkv)


def attention_back(qkv, upstream, lse, kpos, meta, size):
    seq, _, units, blocks, short, lanes = qkv.shape
    slots = kpos.shape[0]
    heads = LANES // HD
    work = units * heads * slots * slots * 5 // 8
    return pl.pallas_call(
        functools.partial(attend_back_kernel, size=size, factor=HD**-0.5),
        grid=(units,),
        in_specs=[
            pl.BlockSpec((slots, 1), lambda r: (0, 0)),
            pl.BlockSpec((None, 2, slots), lambda r: (r, 0, 0)),
            pl.BlockSpec((None, heads, slots), lambda r: (r, 0, 0)),
            *(kind_spec(qkv.shape, kind) for kind in range(3)),
            pl.BlockSpec((seq, None, blocks, short, lanes), lambda r: (0, r, 0, 0, 0)),
        ],
        out_specs=pl.BlockSpec((seq, 3, None, blocks, short, lanes), lambda r: (0, 0, r, 0, 0, 0)),
        out_shape=jax.ShapeDtypeStruct(qkv.shape, BF16),
        scratch_shapes=[pltpu.VMEM((slots, LANES), F32), pltpu.VMEM((slots, LANES), F32)],
        compiler_params=pltpu.CompilerParams(vmem_limit_bytes=48 << 20),
        cost_estimate=pl.CostEstimate(
            flops=work * HD * 10 * 4, bytes_accessed=units * slots * LANES * 16, transcendentals=work
        ),
        name="attend_back",
    )(kpos, meta, lse, qkv, qkv, qkv, upstream)


def per_device(
    layer_in,
    doc_ids,
    cotangent,
    norm_params,
    w_qkv,
    w_out,
    w_up,
    w_down,
    norm_moment,
    norm_average,
    qkv_moment,
    qkv_average,
    out_moment,
    out_average,
    up_moment,
    up_average,
    down_moment,
    down_average,
):
    mdl_count = lax.axis_size("mdl")
    seq_count = lax.axis_size("seq")
    micro, rows, short, width = layer_in.shape
    slots = doc_ids.shape[2]
    slot_dev = short * mdl_count
    embed = w_qkv.shape[2]
    pairs = embed // LANES
    groups = seq_count // pairs
    chunks = CHUNKS
    while (micro * rows // chunks) % groups:
        chunks //= 2
    chunk_rows = micro * rows // chunks
    units = chunk_rows // groups
    size = slot_dev * max(1, 256 // slot_dev)
    seq_index = lax.axis_index("seq")
    mdl_index = lax.axis_index("mdl")

    behind = (mdl_index - jnp.arange(mdl_count, dtype=jnp.int32)) % mdl_count
    order = (
        jnp.arange(seq_count, dtype=jnp.int32)[:, None, None] * slot_dev
        + behind[None, :, None] * short
        + jnp.arange(short, dtype=jnp.int32)
    ).reshape(slots)
    docs = doc_ids.reshape(chunks, groups, units, slots)
    docs = lax.dynamic_index_in_dim(docs, seq_index % groups, 1, False)
    first = jnp.sum(
        ((docs[..., None, :] >= 0) & (docs[..., None, :] < docs[..., :, None])).astype(jnp.int32), -1
    )
    first = jnp.where(docs >= 0, first, jnp.arange(slots, dtype=jnp.int32))
    first = first.reshape(chunks, units, seq_count, mdl_count, short)
    first = jnp.stack(
        [lax.dynamic_index_in_dim(first, behind[j], 3, False) for j in range(mdl_count)], 3
    ).reshape(chunks, units, slots)
    meta = jnp.stack([first, jnp.broadcast_to(order, first.shape)], 2)
    kpos = order[:, None]

    qkv_full = lax.all_gather(w_qkv.astype(BF16), "seq", axis=0, tiled=True).reshape(width, 3 * embed)
    out_full = lax.all_gather(w_out.astype(BF16), "seq", axis=0, tiled=True)
    up_full = lax.all_gather(w_up.astype(BF16), "seq", axis=0, tiled=True)
    down_full = lax.all_gather(w_down.astype(BF16), "seq", axis=0, tiled=True)

    def exchange(value):
        return lax.all_to_all(value, "seq", 0, 0, tiled=True)

    def gather(value):
        return ring_gather(value, "mdl").reshape(-1, width)

    def scatter(value):
        return ring_scatter(value.reshape(mdl_count, chunk_rows * short, width), "mdl")

    def to_units(value, kinds):
        value = value.reshape(mdl_count, groups, units, short, kinds, pairs, LANES)
        value = value.transpose(5, 1, 4, 2, 0, 3, 6)
        return value.reshape(seq_count, kinds, units, mdl_count, short, LANES)

    def from_units(value, kinds):
        value = value.reshape(pairs, groups, kinds, units, mdl_count, short, LANES)
        value = value.transpose(4, 1, 3, 5, 2, 0, 6)
        return value.reshape(mdl_count * chunk_rows * short, kinds * embed)

    span = micro // chunks
    saved = []
    outputs, input_grads = [], []
    norm_sums = jnp.zeros((4, width), F32)
    for c in range(chunks):
        inputs = layer_in[c * span : (c + 1) * span].reshape(-1, width)
        upstream = cotangent[c * span : (c + 1) * span].reshape(-1, width)
        normed_one, hat_one, inv_one = norm_forward(inputs, norm_params[0], norm_params[1])
        rows_one = gather(normed_one.astype(BF16))
        projected = dot(rows_one, qkv_full, ((1,), (0,))).astype(BF16)
        qkv = exchange(to_units(projected, 3))
        out, lse = attention(qkv, kpos, meta[c], size)
        attended = from_units(exchange(out), 1)
        mixed = scatter(dot(attended, out_full, ((1,), (1,))))
        middle = inputs + mixed
        normed_two, hat_two, inv_two = norm_forward(middle, norm_params[2], norm_params[3])
        rows_two = gather(normed_two.astype(BF16))
        up_proj = dot(rows_two, up_full, ((1,), (0,)))
        cdf = 0.5 * (1.0 + lax.erf(up_proj * HALF_ROOT))
        hidden = (up_proj * cdf).astype(BF16)
        slope = cdf + up_proj * jnp.exp(-0.5 * up_proj * up_proj) * INV_ROOT_TWO_PI
        branch = scatter(dot(hidden, down_full, ((1,), (1,))))
        outputs.append(middle + branch)
        back_rows = gather(upstream.astype(BF16))
        hidden_grad = dot(back_rows, down_full, ((1,), (0,)))
        up_back = (hidden_grad * slope).astype(BF16)
        second_in = scatter(dot(up_back, up_full, ((1,), (1,))))
        middle_grad = upstream + norm_backward(second_in, hat_two, inv_two, norm_params[2])
        resid_rows = gather(middle_grad.astype(BF16))
        attended_back = dot(resid_rows, out_full, ((1,), (0,))).astype(BF16)
        unit_back = exchange(to_units(attended_back, 1))[:, 0]
        qkv_back = attention_back(qkv, unit_back, lse, kpos, meta[c], size)
        proj_back = from_units(exchange(qkv_back), 3)
        first_in = scatter(dot(proj_back, qkv_full, ((1,), (1,))))
        input_grads.append(middle_grad + norm_backward(first_in, hat_one, inv_one, norm_params[0]))
        norm_sums = norm_sums + jnp.stack(
            [
                jnp.sum(first_in * hat_one, 0),
                jnp.sum(first_in, 0),
                jnp.sum(second_in * hat_two, 0),
                jnp.sum(second_in, 0),
            ]
        )
        saved.append((rows_one, proj_back, resid_rows, attended, rows_two, up_back, back_rows, hidden))

    whole = [jnp.concatenate(parts, 0) for parts in zip(*saved)]
    rows_one, proj_back, resid_rows, attended, rows_two, up_back, back_rows, hidden = whole

    def grad(left, right):
        return lax.psum_scatter(
            dot(left, right, ((0,), (0,))).astype(BF16), "seq", scatter_dimension=0, tiled=True
        ).astype(F32)

    down_grad = grad(back_rows, hidden)
    up_grad = grad(rows_two, up_back)
    out_grad = grad(resid_rows, attended)
    qkv_grad = grad(rows_one, proj_back).reshape(w_qkv.shape)
    norm_total = lax.psum(norm_sums, ("seq", "mdl"))
    total_tokens = micro * rows * slots
    weight_rate = 0.02 * total_tokens ** (-0.5)
    norm_rate = 0.15 * total_tokens ** (-0.5)
    shape = layer_in.shape
    return (
        jnp.concatenate(outputs, 0).reshape(shape),
        jnp.concatenate(input_grads, 0).reshape(shape),
        *update_param(norm_params, norm_total, norm_moment, norm_average, norm_rate),
        *update_param(w_qkv, qkv_grad, qkv_moment, qkv_average, weight_rate),
        *update_param(w_out, out_grad, out_moment, out_average, weight_rate),
        *update_param(w_up, up_grad, up_moment, up_average, weight_rate),
        *update_param(w_down, down_grad, down_moment, down_average, weight_rate),
    )


def solution(mesh):
    slots = P(None, None, ("seq", "mdl"), None)
    wide = P("seq", None, "mdl")
    flat = P("seq", "mdl")
    return jax.shard_map(
        per_device,
        mesh=mesh,
        in_specs=(
            *(slots, P(), slots, P(), wide, flat, flat, flat),
            *(P(), P(), wide, wide, flat, flat, flat, flat, flat, flat),
        ),
        out_specs=(
            *(slots, slots, P(), P(), P(), P()),
            *(wide,) * 4,
            *(flat,) * 12,
        ),
        check_vma=False,
    )
```

```python
import functools

import jax
import jax.numpy as jnp
from jax import lax
from jax.experimental import pallas as pl
from jax.experimental.pallas import tpu as pltpu
from jax.sharding import PartitionSpec as P

HD = 64
LANES = 128
CHUNKS = 1

EPSILON = 1e-05
HALF_ROOT = 0.7071067811865476
INV_ROOT_TWO_PI = 0.3989422804014327
BF16 = jnp.bfloat16
F32 = jnp.float32


def norm_forward(values, gain, shift):
    row_mean = jnp.mean(values, -1, keepdims=True)
    centred = values - row_mean
    inv_std = lax.rsqrt(jnp.mean(centred * centred, -1, keepdims=True) + EPSILON)
    normed = centred * inv_std
    return (normed * gain + shift, normed, inv_std)


def norm_backward(upstream, normed, inv_std, gain):
    scaled = upstream * gain
    return inv_std * (
        scaled
        - jnp.mean(scaled, -1, keepdims=True)
        - normed * jnp.mean(scaled * normed, -1, keepdims=True)
    )


def update_param(weight, grad, moment, average, rate):
    new_moment = 0.5 * moment + grad
    new_weight = weight - rate * (grad + 0.5 * new_moment)
    new_average = 0.5 * average + 0.5 * new_weight
    return (new_moment, new_average, new_weight, new_weight.astype(BF16))


def dot(a, b, dims):
    return lax.dot_general(a, b, (dims, ((), ())), preferred_element_type=F32)


def tied(value, earlier):
    return lax.optimization_barrier((value, earlier))


def whole_sum(value, axes):
    for axis in axes:
        count = lax.axis_size(axis)
        step = 1
        while step < count:
            value = value + lax.ppermute(value, axis, [(i, i ^ step) for i in range(count)])
            step *= 2
    return value


def score_blocks(keys, queries, kpos, first, last, start, size):
    diag = dot(keys[start : start + size], queries, ((1,), (1,)))
    pos = kpos[start : start + size]
    diag = jnp.where((pos >= first) & (pos <= last), diag, -1e30)
    if not start:
        return [diag]
    ahead = dot(keys[:start], queries, ((1,), (1,)))
    return [jnp.where(kpos[:start] >= first, ahead, -1e30), diag]


def attend_kernel(own_ref, kpos_ref, meta_ref, q_ref, k_ref, v_ref, o_ref, lse_ref, *, size, factor):
    slots = kpos_ref.shape[0]
    count, short = q_ref.shape[1:3]
    per = count * short
    own = own_ref[0]
    heads = LANES // HD
    keys = k_ref[...].reshape(slots, LANES)
    values = v_ref[...].reshape(slots, LANES)
    kpos = kpos_ref[...]
    for start in range(0, slots, size):
        span = pl.ds(start // per, size // per)
        queries = q_ref[span].reshape(size, LANES) * factor
        first = meta_ref[0:1, start : start + size]
        last = meta_ref[1:2, start : start + size]
        outs = []
        for head in range(heads):
            cols = slice(head * HD, (head + 1) * HD)
            blocks = score_blocks(keys[:, cols], queries[:, cols], kpos, first, last, start, size)
            top = functools.reduce(jnp.maximum, [jnp.max(b, 0, keepdims=True) for b in blocks])
            blocks = [jnp.exp(b - top) for b in blocks]
            total = functools.reduce(jnp.add, [jnp.sum(b, 0, keepdims=True) for b in blocks])
            lse_ref[head : head + 1, start : start + size] = top + jnp.log(total)
            inverse = 1.0 / total
            out = None
            offset = 0
            for b in blocks:
                rows = slice(offset, offset + b.shape[0])
                offset += b.shape[0]
                term = dot(values[rows, cols], (b * inverse).astype(BF16), ((0,), (0,)))
                out = term if out is None else out + term
            outs.append(out)
        merged = jnp.concatenate(outs, 0).T.astype(BF16)
        for j in range(count):
            place = lax.rem(own + (count - j), count)
            for k in range(size // per):
                rows = slice(k * per + j * short, k * per + (j + 1) * short)
                o_ref[start // per + k, place] = merged[rows]


def attend_back_kernel(
    own_ref, kpos_ref, meta_ref, lse_ref, q_ref, k_ref, v_ref, g_ref, out_ref, dk_acc, dv_acc, *, size, factor
):
    slots = kpos_ref.shape[0]
    count, short = q_ref.shape[1:3]
    per = count * short
    own = own_ref[0]
    heads = LANES // HD
    keys = k_ref[...].reshape(slots, LANES)
    values = v_ref[...].reshape(slots, LANES)
    kpos = kpos_ref[...]
    dk_acc[...] = jnp.zeros_like(dk_acc)
    dv_acc[...] = jnp.zeros_like(dv_acc)
    for start in range(0, slots, size):
        span = pl.ds(start // per, size // per)
        queries = q_ref[span].reshape(size, LANES) * factor
        upstream = jnp.concatenate(
            [
                g_ref[start // per + k, lax.rem(own + (count - j), count)]
                for k in range(size // per)
                for j in range(count)
            ],
            0,
        )
        first = meta_ref[0:1, start : start + size]
        last = meta_ref[1:2, start : start + size]
        dqs, dks, dvs = [], [], []
        for head in range(heads):
            cols = slice(head * HD, (head + 1) * HD)
            blocks = score_blocks(keys[:, cols], queries[:, cols], kpos, first, last, start, size)
            lse = lse_ref[head : head + 1, start : start + size]
            probs = [jnp.exp(b - lse) for b in blocks]
            edges = [0] + ([start] if start else []) + [start + size]
            rows = [slice(a, b) for a, b in zip(edges[:-1], edges[1:])]
            back = [dot(values[r, cols], upstream[:, cols], ((1,), (1,))) for r in rows]
            terms = [p * b for p, b in zip(probs, back)]
            weighted = functools.reduce(jnp.add, [jnp.sum(t, 0, keepdims=True) for t in terms])
            score_back = [(t - p * weighted).astype(BF16) for t, p in zip(terms, probs)]
            dks.append([dot(s, queries[:, cols], ((1,), (0,))) for s in score_back])
            dvs.append([dot(p.astype(BF16), upstream[:, cols], ((1,), (0,))) for p in probs])
            dq = [dot(keys[r, cols], s, ((0,), (0,))) for r, s in zip(rows, score_back)]
            dqs.append(functools.reduce(jnp.add, dq) * factor)
        merged = jnp.concatenate(dqs, 0).T.astype(BF16)
        out_ref[span, 0] = merged.reshape(size // per, *out_ref.shape[2:])
        for i, r in enumerate(rows):
            dk_acc[r] += jnp.concatenate([d[i] for d in dks], 1)
            dv_acc[r] += jnp.concatenate([d[i] for d in dvs], 1)
    shape = (out_ref.shape[0], *out_ref.shape[2:])
    out_ref[:, 1] = dk_acc[...].astype(BF16).reshape(shape)
    out_ref[:, 2] = dv_acc[...].astype(BF16).reshape(shape)


def kind_spec(shape, kind):
    seq, _, _, blocks, short, lanes = shape
    return pl.BlockSpec(
        (seq, None, None, blocks, short, lanes), lambda r, kind=kind: (0, kind, r, 0, 0, 0)
    )


def attention(own, qkv, kpos, meta, size):
    seq, _, units, blocks, short, lanes = qkv.shape
    slots = kpos.shape[0]
    heads = LANES // HD
    work = units * heads * slots * slots * 5 // 8
    return pl.pallas_call(
        functools.partial(attend_kernel, size=size, factor=HD**-0.5),
        grid=(units,),
        in_specs=[
            pl.BlockSpec(memory_space=pltpu.SMEM),
            pl.BlockSpec((slots, 1), lambda r: (0, 0)),
            pl.BlockSpec((None, 2, slots), lambda r: (r, 0, 0)),
            *(kind_spec(qkv.shape, kind) for kind in range(3)),
        ],
        out_specs=[
            pl.BlockSpec((seq, blocks, None, short, lanes), lambda r: (0, 0, r, 0, 0)),
            pl.BlockSpec((None, heads, slots), lambda r: (r, 0, 0)),
        ],
        out_shape=[
            jax.ShapeDtypeStruct((seq, blocks, units, short, lanes), BF16),
            jax.ShapeDtypeStruct((units, heads, slots), F32),
        ],
        compiler_params=pltpu.CompilerParams(vmem_limit_bytes=48 << 20),
        cost_estimate=pl.CostEstimate(
            flops=work * HD * 4 * 4, bytes_accessed=units * slots * LANES * 8, transcendentals=work
        ),
        name="attend",
    )(own, kpos, meta, qkv, qkv, qkv)


def attention_back(own, qkv, upstream, lse, kpos, meta, size):
    seq, _, units, blocks, short, lanes = qkv.shape
    slots = kpos.shape[0]
    heads = LANES // HD
    work = units * heads * slots * slots * 5 // 8
    return pl.pallas_call(
        functools.partial(attend_back_kernel, size=size, factor=HD**-0.5),
        grid=(units,),
        in_specs=[
            pl.BlockSpec(memory_space=pltpu.SMEM),
            pl.BlockSpec((slots, 1), lambda r: (0, 0)),
            pl.BlockSpec((None, 2, slots), lambda r: (r, 0, 0)),
            pl.BlockSpec((None, heads, slots), lambda r: (r, 0, 0)),
            *(kind_spec(qkv.shape, kind) for kind in range(3)),
            pl.BlockSpec((seq, blocks, None, short, lanes), lambda r: (0, 0, r, 0, 0)),
        ],
        out_specs=pl.BlockSpec((seq, 3, None, blocks, short, lanes), lambda r: (0, 0, r, 0, 0, 0)),
        out_shape=jax.ShapeDtypeStruct(qkv.shape, BF16),
        scratch_shapes=[pltpu.VMEM((slots, LANES), F32), pltpu.VMEM((slots, LANES), F32)],
        compiler_params=pltpu.CompilerParams(vmem_limit_bytes=48 << 20),
        cost_estimate=pl.CostEstimate(
            flops=work * HD * 10 * 4, bytes_accessed=units * slots * LANES * 16, transcendentals=work
        ),
        name="attend_back",
    )(own, kpos, meta, lse, qkv, qkv, qkv, upstream)


def per_device(
    layer_in,
    doc_ids,
    cotangent,
    norm_params,
    w_qkv,
    w_out,
    w_up,
    w_down,
    norm_moment,
    norm_average,
    qkv_moment,
    qkv_average,
    out_moment,
    out_average,
    up_moment,
    up_average,
    down_moment,
    down_average,
):
    mdl_count = lax.axis_size("mdl")
    seq_count = lax.axis_size("seq")
    micro, rows, short, width = layer_in.shape
    slots = doc_ids.shape[2]
    slot_dev = short * mdl_count
    embed = w_qkv.shape[2]
    pairs = embed // LANES
    groups = seq_count // pairs
    chunks = CHUNKS
    while (micro * rows // chunks) % groups:
        chunks //= 2
    chunk_rows = micro * rows // chunks
    units = chunk_rows // groups
    size = slot_dev * max(1, 256 // slot_dev)
    seq_index = lax.axis_index("seq")
    mdl_index = lax.axis_index("mdl")

    behind = (mdl_index - jnp.arange(mdl_count, dtype=jnp.int32)) % mdl_count
    order = (
        jnp.arange(seq_count, dtype=jnp.int32)[:, None, None] * slot_dev
        + behind[None, :, None] * short
        + jnp.arange(short, dtype=jnp.int32)
    ).reshape(slots)
    docs = doc_ids.reshape(chunks, groups, units, slots)
    docs = lax.dynamic_index_in_dim(docs, seq_index % groups, 1, False)
    first = jnp.sum(
        ((docs[..., None, :] >= 0) & (docs[..., None, :] < docs[..., :, None])).astype(jnp.int32), -1
    )
    first = jnp.where(docs >= 0, first, jnp.arange(slots, dtype=jnp.int32))
    first = first.reshape(chunks, units, seq_count, mdl_count, short)
    first = jnp.stack(
        [lax.dynamic_index_in_dim(first, behind[j], 3, False) for j in range(mdl_count)], 3
    ).reshape(chunks, units, slots)
    meta = jnp.stack([first, jnp.broadcast_to(order, first.shape)], 2)
    kpos = order[:, None]
    own = mdl_index.reshape(1).astype(jnp.int32)

    def exchange(value):
        return lax.all_to_all(value, "seq", 0, 0, tiled=True)

    def exchange_all(value):
        shape = (seq_count * mdl_count, units, short, LANES)
        return lax.all_to_all(value.reshape(shape), ("seq", "mdl"), 0, 0, tiled=True)

    def own_heads(value):
        value = value.reshape(pairs, groups, mdl_count, units, short, LANES)
        return value.transpose(1, 3, 4, 2, 0, 5).reshape(chunk_rows * short, mdl_count * embed)

    def own_units(value):
        value = value.reshape(groups, units, short, mdl_count, pairs, LANES)
        return value.transpose(4, 0, 3, 1, 2, 5).reshape(-1, units, short, LANES)

    def to_units(value, kinds):
        value = value.reshape(mdl_count, groups, units, short, kinds, pairs, LANES)
        value = value.transpose(5, 1, 4, 2, 0, 3, 6)
        return value.reshape(seq_count, kinds, units, mdl_count, short, LANES)

    def from_units(value, kinds):
        value = value.reshape(pairs, groups, kinds, units, mdl_count, short, LANES)
        value = value.transpose(4, 1, 3, 5, 2, 0, 6)
        return value.reshape(mdl_count * chunk_rows * short, kinds * embed)

    ring = [(i, (i + 1) % mdl_count) for i in range(mdl_count)]
    members = range(mdl_count)
    tokens = micro * rows * short

    def pass_on(value):
        return lax.ppermute(value, "mdl", ring)

    held = {}

    def behind(value, *names):
        for name in names:
            value, held[name] = tied(value, held[name])
        return value

    def ring_gather(value, gates=()):
        parts = [value]
        for j in members[1:]:
            ahead = parts[-1]
            if j <= len(gates) and gates[j - 1]:
                ahead = behind(ahead, gates[j - 1])
            parts.append(pass_on(ahead))
        return parts

    def ring_terms(parts):
        carried = None
        for j in members[1:]:
            term = parts[j] if carried is None else parts[j] + carried.astype(F32)
            carried = yield term.astype(BF16)

    def ring_scatter(parts):
        terms = ring_terms(parts)
        term = next(terms)
        while True:
            carried = pass_on(term)
            try:
                term = terms.send(carried)
            except StopIteration:
                return carried

    def spread(weight):
        return lax.all_gather(weight, "seq", axis=0, tiled=True)

    def by_member(parts):
        placed = []
        for k in members:
            turns = (mdl_index - k) % mdl_count
            value = parts[0]
            for j in members[1:]:
                value = jnp.where(turns == j, parts[j], value)
            placed.append(value)
        return jnp.concatenate(placed, 1)

    def grad(left, right):
        return dot(left, right, ((0,), (0,))).astype(BF16)

    chips = seq_count // 2
    cycle = [*range(0, chips, 2), *range(chips - 1, 0, -2)]
    swap = [(i, i ^ 1) for i in range(seq_count)]
    onward, blocks_behind = [], []
    for index in range(seq_count):
        place, way = cycle.index(index // 2), 1 - 2 * (index % 2)
        onward.append((index, 2 * cycle[(place + way) % chips] + index % 2))
        blocks_behind.append([cycle[(place - way * j) % chips] for j in range(chips)])
    blocks_behind = lax.dynamic_index_in_dim(
        jnp.array(blocks_behind, jnp.int32), seq_index, 0, False
    )
    core = seq_index % 2

    def shared(value):
        return lax.psum_scatter(value, "seq", scatter_dimension=0, tiled=True).astype(F32)

    def share(value):
        value = value.reshape(chips, 2, -1, value.shape[-1])
        other = lax.ppermute(lax.dynamic_index_in_dim(value, 1 - core, 1, False), "seq", swap)

        def term(j):
            block = blocks_behind[j]
            zero = jnp.zeros_like(block)
            mine = lax.dynamic_slice(
                value, (block, core, zero, zero), (1, 1, *value.shape[2:])
            ).reshape(value.shape[2:])
            return mine.astype(F32) + lax.dynamic_index_in_dim(other, block, 0, False).astype(F32)

        carried = lax.ppermute(term(1).astype(BF16), "seq", onward)
        for j in range(2, chips):
            carried = lax.ppermute((term(j) + carried.astype(F32)).astype(BF16), "seq", onward)
        return term(0) + carried.astype(F32)

    total_tokens = micro * rows * slots
    weight_rate = 0.02 * total_tokens ** (-0.5)
    norm_rate = 0.15 * total_tokens ** (-0.5)
    each = range(chunks)
    inputs = layer_in.reshape(tokens, width)
    upstream = cotangent.reshape(tokens, width)

    low_qkv = w_qkv.astype(BF16).reshape(-1, 3 * embed)
    normed, hat_one, inv_one = norm_forward(inputs, norm_params[0], norm_params[1])
    normed, low_qkv = tied(normed.astype(BF16), low_qkv)
    full_qkv = spread(low_qkv)
    rows_one = ring_gather(normed)
    low_up, full_qkv = tied(w_up.astype(BF16), full_qkv)
    full_up = spread(low_up)
    projected = [dot(part, full_qkv, ((1,), (0,))).astype(BF16) for part in rows_one]
    low_out, projected = tied(w_out.astype(BF16), projected)
    full_out = spread(lax.all_gather(low_out, "mdl", axis=1, tiled=True))
    projected = jnp.stack(projected).reshape(mdl_count, chunks, -1, 3 * embed)
    held["one"] = rows_one[-1]
    held["qkv"] = [exchange(to_units(projected[:, c], 3)) for c in each]
    back = behind(upstream.astype(BF16), "one")
    rows_one[-1] = held["one"]
    rows_back = [back, pass_on(back)]
    rows_back.append(pass_on(behind(rows_back[-1], "qkv")))

    seen = [attention(own, held["qkv"][c], kpos, meta[c], size) for c in each]
    held["seen"] = seen
    full_down = spread(behind(w_down.astype(BF16), "seen"))
    for _ in members[3:]:
        rows_back.append(pass_on(behind(rows_back[-1], "seen")))
    seen = held["seen"]
    attended = [own_heads(exchange_all(value[0])) for value in seen]
    attended = jnp.concatenate(attended, 0)
    middle = inputs + dot(attended, full_out, ((1,), (1,)))
    normed, hat_two, inv_two = norm_forward(middle, norm_params[2], norm_params[3])
    normed = normed.astype(BF16)
    normed, rows_back[-1] = tied(normed, rows_back[-1])

    rows_two = ring_gather(normed)
    hidden, up_back, second = [], [], []
    for j in members:
        up_proj = dot(rows_two[j], full_up, ((1,), (0,)))
        cdf = 0.5 * (1.0 + lax.erf(up_proj * HALF_ROOT))
        slope = cdf + up_proj * jnp.exp(-0.5 * up_proj * up_proj) * INV_ROOT_TWO_PI
        hidden.append((up_proj * cdf).astype(BF16))
        up_back.append((dot(rows_back[j], full_down, ((1,), (0,))) * slope).astype(BF16))
        second.append(dot(up_back[j], full_up, ((1,), (1,))))
    second_sum = ring_scatter(second)
    branch = [dot(value, full_down, ((1,), (1,))) for value in hidden]
    down_part = grad(jnp.concatenate(rows_back, 0), jnp.concatenate(hidden, 0))
    up_part = grad(jnp.concatenate(rows_two, 0), jnp.concatenate(up_back, 0))
    second_sum, (down_part, up_part, branch) = tied(second_sum, (down_part, up_part, branch))
    held["down"], held["up"] = shared(down_part), shared(up_part)
    second_in = second[0] + second_sum.astype(F32)
    middle_grad = upstream + norm_backward(second_in, hat_two, inv_two, norm_params[2])
    middle_low = middle_grad.astype(BF16)

    attended_back = dot(middle_low, full_out, ((1,), (0,))).astype(BF16)
    held["back"] = attended_back
    terms = ring_terms(branch)
    carried = pass_on(next(terms))
    attended_back = held["back"].reshape(chunks, -1, mdl_count * embed)
    held["unit"] = [exchange_all(own_units(attended_back[c])) for c in each]
    carried = pass_on(terms.send(behind(carried, "unit")))
    held["out"] = shared(grad(behind(middle_low, "unit"), attended))
    held["attg"] = [
        attention_back(
            own,
            held["qkv"][c],
            held["unit"][c].reshape(seq_count, mdl_count, units, short, LANES),
            held["seen"][c][1],
            kpos,
            meta[c],
            size,
        )
        for c in each
    ]
    for _ in members[3:]:
        carried = pass_on(terms.send(behind(carried, "attg")))
    proj_back = [
        from_units(exchange(value), 3).reshape(mdl_count, -1, 3 * embed) for value in held["attg"]
    ]
    proj_back = jnp.concatenate(proj_back, 1)
    proj_back = behind(proj_back, "down")
    proj_back, carried = tied(proj_back, carried)
    layer_out = middle + (branch[0] + carried.astype(F32))
    first = [dot(proj_back[j], full_qkv, ((1,), (1,))) for j in members]
    proj_back, first[1] = tied(proj_back.reshape(-1, 3 * embed), first[1])
    first_sum = ring_scatter(first)
    held["qkv_grad"] = share(grad(jnp.concatenate(rows_one, 0), proj_back))
    columns = [
        lax.dynamic_slice_in_dim(held["out"], embed * ((mdl_index - j) % mdl_count), embed, 1)
        for j in members
    ]
    held["out_grad"] = columns[0] + ring_scatter(columns).astype(F32)
    first_sum = behind(first_sum, "up", "out_grad", "qkv_grad")
    down_grad, up_grad = held["down"], held["up"]
    out_grad, qkv_grad = held["out_grad"], held["qkv_grad"]
    first_in = first[0] + first_sum.astype(F32)
    input_grad = middle_grad + norm_backward(first_in, hat_one, inv_one, norm_params[0])
    norm_total = whole_sum(
        jnp.stack(
            [
                jnp.sum(first_in * hat_one, 0),
                jnp.sum(first_in, 0),
                jnp.sum(second_in * hat_two, 0),
                jnp.sum(second_in, 0),
            ]
        ),
        ("mdl", "seq"),
    )
    def updated(weight, total, moment, average):
        if weight.ndim == 2:
            return update_param(weight, total, moment, average, weight_rate)
        kinds = [value.swapaxes(0, 1) for value in (weight, moment, average)]
        total = jnp.stack(jnp.split(total, 3, 1))
        new = update_param(kinds[0], total, *kinds[1:], weight_rate)
        return [value.swapaxes(0, 1) for value in new]

    shape = layer_in.shape
    return (
        layer_out.reshape(shape),
        input_grad.reshape(shape),
        *update_param(norm_params, norm_total, norm_moment, norm_average, norm_rate),
        *updated(w_qkv, qkv_grad, qkv_moment, qkv_average),
        *updated(w_out, out_grad, out_moment, out_average),
        *updated(w_up, up_grad, up_moment, up_average),
        *updated(w_down, down_grad, down_moment, down_average),
    )


def solution(mesh):
    slots = P(None, None, ("seq", "mdl"), None)
    wide = P("seq", None, "mdl")
    flat = P("seq", "mdl")
    return jax.shard_map(
        per_device,
        mesh=mesh,
        in_specs=(
            *(slots, P(), slots, P(), wide, flat, flat, flat),
            *(P(), P(), wide, wide, flat, flat, flat, flat, flat, flat),
        ),
        out_specs=(
            *(slots, slots, P(), P(), P(), P()),
            *(wide,) * 4,
            *(flat,) * 12,
        ),
        check_vma=False,
    )
```

```python
import functools
import itertools

import jax
import jax.numpy as jnp
from jax import lax
from jax.experimental import pallas as pl
from jax.experimental.pallas import tpu as pltpu
from jax.sharding import PartitionSpec as P

HD = 64
LANES = 128

EPSILON = 1e-05
HALF_ROOT = 0.7071067811865476
INV_ROOT_TWO_PI = 0.3989422804014327
BF16 = jnp.bfloat16
F32 = jnp.float32


def norm_forward(values, gain, shift):
    row_mean = jnp.mean(values, -1, keepdims=True)
    centred = values - row_mean
    inv_std = lax.rsqrt(jnp.mean(centred * centred, -1, keepdims=True) + EPSILON)
    normed = centred * inv_std
    return (normed * gain + shift, normed, inv_std)


def norm_backward(upstream, normed, inv_std, gain):
    scaled = upstream * gain
    return inv_std * (
        scaled
        - jnp.mean(scaled, -1, keepdims=True)
        - normed * jnp.mean(scaled * normed, -1, keepdims=True)
    )


def update_param(weight, grad, moment, average, rate):
    new_moment = 0.5 * moment + grad
    new_weight = weight - rate * (grad + 0.5 * new_moment)
    new_average = 0.5 * average + 0.5 * new_weight
    return (new_moment, new_average, new_weight, new_weight.astype(BF16))


def dot(a, b, dims):
    return lax.dot_general(a, b, (dims, ((), ())), preferred_element_type=F32)


def tied(value, earlier):
    return lax.optimization_barrier((value, earlier))


def whole_sum(value, axes):
    for axis in axes:
        count = lax.axis_size(axis)
        step = 1
        while step < count:
            value = value + lax.ppermute(value, axis, [(i, i ^ step) for i in range(count)])
            step *= 2
    return value


def score_blocks(keys, queries, kpos, first, last, start, size):
    diag = dot(keys[start : start + size], queries, ((1,), (1,)))
    pos = kpos[start : start + size]
    diag = jnp.where((pos >= first) & (pos <= last), diag, -1e30)
    if not start:
        return [diag]
    ahead = dot(keys[:start], queries, ((1,), (1,)))
    return [jnp.where(kpos[:start] >= first, ahead, -1e30), diag]


def attend_kernel(own_ref, kpos_ref, meta_ref, q_ref, k_ref, v_ref, o_ref, lse_ref, *, size, factor):
    slots = kpos_ref.shape[0]
    count, short = q_ref.shape[1:3]
    per = count * short
    own = own_ref[0]
    heads = LANES // HD
    keys = k_ref[...].reshape(slots, LANES)
    values = v_ref[...].reshape(slots, LANES)
    kpos = kpos_ref[...]
    for start in range(0, slots, size):
        span = pl.ds(start // per, size // per)
        queries = q_ref[span].reshape(size, LANES) * factor
        first = meta_ref[0:1, start : start + size]
        last = meta_ref[1:2, start : start + size]
        outs = []
        for head in range(heads):
            cols = slice(head * HD, (head + 1) * HD)
            blocks = score_blocks(keys[:, cols], queries[:, cols], kpos, first, last, start, size)
            top = functools.reduce(jnp.maximum, [jnp.max(b, 0, keepdims=True) for b in blocks])
            blocks = [jnp.exp(b - top) for b in blocks]
            total = functools.reduce(jnp.add, [jnp.sum(b, 0, keepdims=True) for b in blocks])
            lse_ref[head : head + 1, start : start + size] = top + jnp.log(total)
            inverse = 1.0 / total
            out = None
            offset = 0
            for b in blocks:
                rows = slice(offset, offset + b.shape[0])
                offset += b.shape[0]
                term = dot(values[rows, cols], (b * inverse).astype(BF16), ((0,), (0,)))
                out = term if out is None else out + term
            outs.append(out)
        merged = jnp.concatenate(outs, 0).T.astype(BF16)
        for j in range(count):
            place = lax.rem(own + (count - j), count)
            for k in range(size // per):
                rows = slice(k * per + j * short, k * per + (j + 1) * short)
                o_ref[start // per + k, place] = merged[rows]


def attend_back_kernel(
    own_ref, kpos_ref, meta_ref, lse_ref, q_ref, k_ref, v_ref, g_ref, out_ref, dk_acc, dv_acc, *, size, factor
):
    slots = kpos_ref.shape[0]
    count, short = q_ref.shape[1:3]
    per = count * short
    own = own_ref[0]
    heads = LANES // HD
    keys = k_ref[...].reshape(slots, LANES)
    values = v_ref[...].reshape(slots, LANES)
    kpos = kpos_ref[...]
    dk_acc[...] = jnp.zeros_like(dk_acc)
    dv_acc[...] = jnp.zeros_like(dv_acc)
    for start in range(0, slots, size):
        span = pl.ds(start // per, size // per)
        queries = q_ref[span].reshape(size, LANES) * factor
        upstream = jnp.concatenate(
            [
                g_ref[start // per + k, lax.rem(own + (count - j), count)]
                for k in range(size // per)
                for j in range(count)
            ],
            0,
        )
        first = meta_ref[0:1, start : start + size]
        last = meta_ref[1:2, start : start + size]
        dqs, dks, dvs = [], [], []
        for head in range(heads):
            cols = slice(head * HD, (head + 1) * HD)
            blocks = score_blocks(keys[:, cols], queries[:, cols], kpos, first, last, start, size)
            lse = lse_ref[head : head + 1, start : start + size]
            probs = [jnp.exp(b - lse) for b in blocks]
            edges = [0] + ([start] if start else []) + [start + size]
            rows = [slice(a, b) for a, b in zip(edges[:-1], edges[1:])]
            back = [dot(values[r, cols], upstream[:, cols], ((1,), (1,))) for r in rows]
            terms = [p * b for p, b in zip(probs, back)]
            weighted = functools.reduce(jnp.add, [jnp.sum(t, 0, keepdims=True) for t in terms])
            score_back = [(t - p * weighted).astype(BF16) for t, p in zip(terms, probs)]
            dks.append([dot(s, queries[:, cols], ((1,), (0,))) for s in score_back])
            dvs.append([dot(p.astype(BF16), upstream[:, cols], ((1,), (0,))) for p in probs])
            dq = [dot(keys[r, cols], s, ((0,), (0,))) for r, s in zip(rows, score_back)]
            dqs.append(functools.reduce(jnp.add, dq) * factor)
        merged = jnp.concatenate(dqs, 0).T.astype(BF16)
        out_ref[span, 0] = merged.reshape(size // per, *out_ref.shape[2:])
        for i, r in enumerate(rows):
            dk_acc[r] += jnp.concatenate([d[i] for d in dks], 1)
            dv_acc[r] += jnp.concatenate([d[i] for d in dvs], 1)
    shape = (out_ref.shape[0], *out_ref.shape[2:])
    out_ref[:, 1] = dk_acc[...].astype(BF16).reshape(shape)
    out_ref[:, 2] = dv_acc[...].astype(BF16).reshape(shape)


def kind_spec(shape, kind):
    seq, _, _, blocks, short, lanes = shape
    return pl.BlockSpec(
        (seq, None, None, blocks, short, lanes), lambda r, kind=kind: (0, kind, r, 0, 0, 0)
    )


def attention(own, qkv, kpos, meta, size):
    seq, _, units, blocks, short, lanes = qkv.shape
    slots = kpos.shape[0]
    heads = LANES // HD
    work = units * heads * slots * slots * 5 // 8
    return pl.pallas_call(
        functools.partial(attend_kernel, size=size, factor=HD**-0.5),
        grid=(units,),
        in_specs=[
            pl.BlockSpec(memory_space=pltpu.SMEM),
            pl.BlockSpec((slots, 1), lambda r: (0, 0)),
            pl.BlockSpec((None, 2, slots), lambda r: (r, 0, 0)),
            *(kind_spec(qkv.shape, kind) for kind in range(3)),
        ],
        out_specs=[
            pl.BlockSpec((seq, blocks, None, short, lanes), lambda r: (0, 0, r, 0, 0)),
            pl.BlockSpec((None, heads, slots), lambda r: (r, 0, 0)),
        ],
        out_shape=[
            jax.ShapeDtypeStruct((seq, blocks, units, short, lanes), BF16),
            jax.ShapeDtypeStruct((units, heads, slots), F32),
        ],
        compiler_params=pltpu.CompilerParams(vmem_limit_bytes=48 << 20),
        cost_estimate=pl.CostEstimate(
            flops=work * HD * 4 * 4, bytes_accessed=units * slots * LANES * 8, transcendentals=work
        ),
        name="attend",
    )(own, kpos, meta, qkv, qkv, qkv)


def attention_back(own, qkv, upstream, lse, kpos, meta, size):
    seq, _, units, blocks, short, lanes = qkv.shape
    slots = kpos.shape[0]
    heads = LANES // HD
    work = units * heads * slots * slots * 5 // 8
    return pl.pallas_call(
        functools.partial(attend_back_kernel, size=size, factor=HD**-0.5),
        grid=(units,),
        in_specs=[
            pl.BlockSpec(memory_space=pltpu.SMEM),
            pl.BlockSpec((slots, 1), lambda r: (0, 0)),
            pl.BlockSpec((None, 2, slots), lambda r: (r, 0, 0)),
            pl.BlockSpec((None, heads, slots), lambda r: (r, 0, 0)),
            *(kind_spec(qkv.shape, kind) for kind in range(3)),
            pl.BlockSpec((seq, blocks, None, short, lanes), lambda r: (0, 0, r, 0, 0)),
        ],
        out_specs=pl.BlockSpec((seq, 3, None, blocks, short, lanes), lambda r: (0, 0, r, 0, 0, 0)),
        out_shape=jax.ShapeDtypeStruct(qkv.shape, BF16),
        scratch_shapes=[pltpu.VMEM((slots, LANES), F32), pltpu.VMEM((slots, LANES), F32)],
        compiler_params=pltpu.CompilerParams(vmem_limit_bytes=48 << 20),
        cost_estimate=pl.CostEstimate(
            flops=work * HD * 10 * 4, bytes_accessed=units * slots * LANES * 16, transcendentals=work
        ),
        name="attend_back",
    )(own, kpos, meta, lse, qkv, qkv, qkv, upstream)


def place_kernel(*refs, moves):
    *sources, target = refs
    for which, source, destination in moves:
        target[destination] = sources[which][source]


def placed(values, shape, moves, name):
    size = 2 * values[0].size * len(values)
    return pl.pallas_call(
        functools.partial(place_kernel, moves=moves),
        in_specs=[pl.BlockSpec(memory_space=pltpu.VMEM)] * len(values),
        out_specs=pl.BlockSpec(memory_space=pltpu.VMEM),
        out_shape=jax.ShapeDtypeStruct(shape, BF16),
        compiler_params=pltpu.CompilerParams(vmem_limit_bytes=32 << 20),
        cost_estimate=pl.CostEstimate(flops=0, bytes_accessed=2 * size, transcendentals=0),
        name=name,
    )(*values)


def per_device(
    layer_in,
    doc_ids,
    cotangent,
    norm_params,
    w_qkv,
    w_out,
    w_up,
    w_down,
    norm_moment,
    norm_average,
    qkv_moment,
    qkv_average,
    out_moment,
    out_average,
    up_moment,
    up_average,
    down_moment,
    down_average,
):
    mdl_count = lax.axis_size("mdl")
    seq_count = lax.axis_size("seq")
    micro, rows, short, width = layer_in.shape
    slots = doc_ids.shape[2]
    slot_dev = short * mdl_count
    embed = w_qkv.shape[2]
    pairs = embed // LANES
    groups = seq_count // pairs
    units = micro * rows // groups
    tokens = micro * rows * short
    size = slot_dev * max(1, 256 // slot_dev)
    seq_index = lax.axis_index("seq")
    mdl_index = lax.axis_index("mdl")

    behind = (mdl_index - jnp.arange(mdl_count, dtype=jnp.int32)) % mdl_count
    order = (
        jnp.arange(seq_count, dtype=jnp.int32)[:, None, None] * slot_dev
        + behind[None, :, None] * short
        + jnp.arange(short, dtype=jnp.int32)
    ).reshape(slots)
    docs = doc_ids.reshape(groups, units, slots)
    docs = lax.dynamic_index_in_dim(docs, seq_index % groups, 0, False)
    first = jnp.sum(
        ((docs[..., None, :] >= 0) & (docs[..., None, :] < docs[..., :, None])).astype(jnp.int32), -1
    )
    first = jnp.where(docs >= 0, first, jnp.arange(slots, dtype=jnp.int32))
    first = first.reshape(units, seq_count, mdl_count, short)
    first = jnp.stack(
        [lax.dynamic_index_in_dim(first, behind[j], 2, False) for j in range(mdl_count)], 2
    ).reshape(units, slots)
    meta = jnp.stack([first, jnp.broadcast_to(order, first.shape)], 1)
    kpos = order[:, None]
    own = mdl_index.reshape(1).astype(jnp.int32)

    def exchange(value):
        return lax.all_to_all(value, "seq", 0, 0, tiled=True)

    def exchange_all(value):
        shape = (seq_count * mdl_count, units, short, LANES)
        return lax.all_to_all(value.reshape(shape), ("seq", "mdl"), 0, 0, tiled=True)

    def row_tile(group, unit):
        start = (group * units + unit) * short
        return slice(start, start + short)

    def column_tile(index, pair):
        start = (index * pairs + pair) * LANES
        return slice(start, start + LANES)

    spots = list(itertools.product(range(groups), range(units), range(pairs)))

    def own_heads(value):
        moves = [
            (0, ((p * groups + g) * mdl_count + m, u), (row_tile(g, u), column_tile(m, p)))
            for g, u, p in spots
            for m in range(mdl_count)
        ]
        return placed([value], (tokens, mdl_count * embed), moves, "own_heads")

    def own_units(value):
        moves = [
            (0, (row_tile(g, u), column_tile(m, p)), ((p * groups + g) * mdl_count + m, u))
            for g, u, p in spots
            for m in range(mdl_count)
        ]
        shape = (seq_count * mdl_count, units, short, LANES)
        return placed([value], shape, moves, "own_units")

    def to_units(values):
        moves = [
            (j, (row_tile(g, u), column_tile(k, p)), (p * groups + g, k, u, j))
            for g, u, p in spots
            for k in range(3)
            for j in range(mdl_count)
        ]
        shape = (seq_count, 3, units, mdl_count, short, LANES)
        return placed(values, shape, moves, "to_units")

    def from_units(value):
        moves = [
            (0, (p * groups + g, k, u, j), (j, row_tile(g, u), column_tile(k, p)))
            for g, u, p in spots
            for k in range(3)
            for j in range(mdl_count)
        ]
        return placed([value], (mdl_count, tokens, 3 * embed), moves, "from_units")

    ring = [(i, (i + 1) % mdl_count) for i in range(mdl_count)]
    members = range(mdl_count)

    def pass_on(value):
        return lax.ppermute(value, "mdl", ring)

    held = {}

    def behind(value, *names):
        for name in names:
            value, held[name] = tied(value, held[name])
        return value

    def ring_gather(value, gates=()):
        parts = [value]
        for j in members[1:]:
            ahead = parts[-1]
            if j <= len(gates) and gates[j - 1]:
                ahead = behind(ahead, gates[j - 1])
            parts.append(pass_on(ahead))
        return parts

    def ring_terms(parts):
        carried = None
        for j in members[1:]:
            term = parts[j] if carried is None else parts[j] + carried.astype(F32)
            carried = yield term.astype(BF16)

    def ring_scatter(parts):
        terms = ring_terms(parts)
        term = next(terms)
        while True:
            carried = pass_on(term)
            try:
                term = terms.send(carried)
            except StopIteration:
                return carried

    def spread(weight):
        return lax.all_gather(weight, "seq", axis=0, tiled=True)

    def by_member(parts):
        placed = []
        for k in members:
            turns = (mdl_index - k) % mdl_count
            value = parts[0]
            for j in members[1:]:
                value = jnp.where(turns == j, parts[j], value)
            placed.append(value)
        return jnp.concatenate(placed, 1)

    def grad(left, right):
        return dot(left, right, ((0,), (0,))).astype(BF16)

    chips = seq_count // 2
    cycle = [*range(0, chips, 2), *range(chips - 1, 0, -2)]
    swap = [(i, i ^ 1) for i in range(seq_count)]
    onward, blocks_behind = [], []
    for index in range(seq_count):
        place, way = cycle.index(index // 2), 1 - 2 * (index % 2)
        onward.append((index, 2 * cycle[(place + way) % chips] + index % 2))
        blocks_behind.append([cycle[(place - way * j) % chips] for j in range(chips)])
    blocks_behind = lax.dynamic_index_in_dim(
        jnp.array(blocks_behind, jnp.int32), seq_index, 0, False
    )
    core = seq_index % 2

    def shared(value):
        return lax.psum_scatter(value, "seq", scatter_dimension=0, tiled=True).astype(F32)

    def share(value):
        value = value.reshape(chips, 2, -1, value.shape[-1])
        other = lax.ppermute(lax.dynamic_index_in_dim(value, 1 - core, 1, False), "seq", swap)

        def term(j):
            block = blocks_behind[j]
            zero = jnp.zeros_like(block)
            mine = lax.dynamic_slice(
                value, (block, core, zero, zero), (1, 1, *value.shape[2:])
            ).reshape(value.shape[2:])
            return mine.astype(F32) + lax.dynamic_index_in_dim(other, block, 0, False).astype(F32)

        carried = lax.ppermute(term(1).astype(BF16), "seq", onward)
        for j in range(2, chips):
            carried = lax.ppermute((term(j) + carried.astype(F32)).astype(BF16), "seq", onward)
        return term(0) + carried.astype(F32)

    total_tokens = micro * rows * slots
    weight_rate = 0.02 * total_tokens ** (-0.5)
    norm_rate = 0.15 * total_tokens ** (-0.5)
    inputs = layer_in.reshape(tokens, width)
    upstream = cotangent.reshape(tokens, width)

    low_qkv = w_qkv.astype(BF16).reshape(-1, 3 * embed)
    normed, hat_one, inv_one = norm_forward(inputs, norm_params[0], norm_params[1])
    normed, low_qkv = tied(normed.astype(BF16), low_qkv)
    full_qkv = spread(low_qkv)
    rows_one = ring_gather(normed)
    low_out, (full_qkv, rows_one[1]) = tied(w_out.astype(BF16), (full_qkv, rows_one[1]))
    wide = lax.all_gather(low_out, "mdl", axis=1, tiled=True)
    wide, rows_one[-1] = tied(wide, rows_one[-1])
    full_out = spread(wide)
    units_in = to_units([dot(part, full_qkv, ((1,), (0,))).astype(BF16) for part in rows_one])
    low_up, units_in = tied(w_up.astype(BF16), units_in)
    full_up = spread(low_up)
    held["one"] = rows_one[-1]
    back = behind(upstream.astype(BF16), "one")
    rows_one[-1] = held["one"]
    rows_back = [back, pass_on(back)]
    qkv = exchange(units_in)
    for j in members[2:]:
        rows_back.append(pass_on(rows_back[-1]))
    qkv, rows_back[-2] = tied(qkv, rows_back[-2])
    rows_back[-1] = pass_on(rows_back[-2])

    heads, lse = attention(own, qkv, kpos, meta, size)
    low_down, held["lse"] = tied(w_down.astype(BF16), lse)
    full_down = spread(low_down)
    heads = exchange_all(heads)
    heads, (full_up, rows_back[-1]) = tied(heads, (full_up, rows_back[-1]))
    attended = own_heads(heads)
    middle = inputs + dot(attended, full_out, ((1,), (1,)))
    normed, hat_two, inv_two = norm_forward(middle, norm_params[2], norm_params[3])
    normed = normed.astype(BF16)

    rows_two = [normed]
    hidden, up_back, second = [None] * mdl_count, [None] * mdl_count, [None] * mdl_count

    def feed(j):
        up_proj = dot(rows_two[j], full_up, ((1,), (0,)))
        cdf = 0.5 * (1.0 + lax.erf(up_proj * HALF_ROOT))
        slope = cdf + up_proj * jnp.exp(-0.5 * up_proj * up_proj) * INV_ROOT_TWO_PI
        hidden[j] = (up_proj * cdf).astype(BF16)
        up_back[j] = (dot(rows_back[j], full_down, ((1,), (0,))) * slope).astype(BF16)
        second[j] = dot(up_back[j], full_up, ((1,), (1,)))

    for j in members[1:]:
        ahead = rows_two[-1]
        if j > 2:
            ahead, hidden[j - 2] = tied(ahead, hidden[j - 2])
            rows_two[-1] = ahead
        rows_two.append(pass_on(ahead))
        feed(j)
    feed(0)
    terms = ring_terms(second)
    term = next(terms)
    for j in members[2:]:
        carried = pass_on(term)
        term = terms.send(carried)
        if j == 2:
            rows_back[0], term = tied(rows_back[0], term)
    rows_two[0], term = tied(rows_two[0], term)
    second_sum = pass_on(term)
    down_part = grad(jnp.concatenate(rows_back, 0), jnp.concatenate(hidden, 0))
    up_part = grad(jnp.concatenate(rows_two, 0), jnp.concatenate(up_back, 0))
    second_sum, (down_part, up_part) = tied(second_sum, (down_part, up_part))
    held["down"] = shared(down_part)
    second_in = second[0] + second_sum.astype(F32)
    middle_grad = upstream + norm_backward(second_in, hat_two, inv_two, norm_params[2])
    middle_low = middle_grad.astype(BF16)

    attended_back = dot(middle_low, full_out, ((1,), (0,))).astype(BF16)
    hidden, attended_back = tied(hidden, attended_back)
    branch = [dot(value, full_down, ((1,), (1,))) for value in hidden]
    held["unit"] = exchange_all(own_units(attended_back))
    branch_terms = ring_terms(branch)
    held["unit"], branch[:] = tied(held["unit"], branch)
    carried = pass_on(behind(next(branch_terms), "unit"))
    out_part = grad(behind(middle_low, "unit"), attended)
    held["attg"] = attention_back(
        own,
        qkv,
        held["unit"].reshape(seq_count, mdl_count, units, short, LANES),
        held["lse"],
        kpos,
        meta,
        size,
    )
    for _ in members[2:-1]:
        carried = pass_on(branch_terms.send(behind(carried, "attg")))
    proj_back = from_units(exchange(held["attg"]))
    proj_back, (up_part, out_part) = tied(proj_back, (up_part, out_part))
    held["out"] = shared(out_part)
    first = [dot(proj_back[j], full_qkv, ((1,), (1,))) for j in members]
    first_terms = ring_terms(first)
    term = next(first_terms)
    (proj_back, up_part), term = tied((proj_back.reshape(-1, 3 * embed), up_part), term)
    held["up"] = shared(up_part)
    first_sum, first[:] = tied(pass_on(term), first)
    qkv_part = grad(jnp.concatenate(rows_one, 0), proj_back)
    term = first_terms.send(first_sum)
    for _ in members[3:]:
        term = first_terms.send(pass_on(term))
    first_sum, qkv_part = tied(pass_on(term), qkv_part)
    held["qkv_grad"] = share(qkv_part)
    columns = jnp.stack(jnp.split(held["out"].astype(BF16), mdl_count, 1))
    columns = lax.all_to_all(columns, "mdl", 0, 0, tiled=True)
    held["out_grad"] = jnp.sum(columns.astype(F32), 0)
    second_late, first[0] = tied((second_in, hat_two), first[0])
    second_sums = [jnp.sum(second_late[0] * second_late[1], 0), jnp.sum(second_late[0], 0)]
    held["sums"] = second_sums
    first_sum = behind(first_sum, "down", "sums")
    carried, first_sum = tied(carried, first_sum)
    carried = pass_on(branch_terms.send(carried))
    layer_out = middle + (branch[0] + carried.astype(F32))
    down_grad, up_grad = held["down"], held["up"]
    out_grad, qkv_grad = held["out_grad"], held["qkv_grad"]
    first_in = first[0] + first_sum.astype(F32)
    input_grad = middle_grad + norm_backward(first_in, hat_one, inv_one, norm_params[0])
    norm_sums = jnp.stack(
        [jnp.sum(first_in * hat_one, 0), jnp.sum(first_in, 0), *held["sums"]]
    )
    norm_sums, (qkv_grad, out_grad, layer_out) = tied(norm_sums, (qkv_grad, out_grad, layer_out))
    norm_total = whole_sum(norm_sums, ("mdl", "seq"))

    def updated(weight, total, moment, average):
        if weight.ndim == 2:
            return update_param(weight, total, moment, average, weight_rate)
        kinds = [value.swapaxes(0, 1) for value in (weight, moment, average)]
        total = jnp.stack(jnp.split(total, 3, 1))
        new = update_param(kinds[0], total, *kinds[1:], weight_rate)
        return [value.swapaxes(0, 1) for value in new]

    shape = layer_in.shape
    return (
        layer_out.reshape(shape),
        input_grad.reshape(shape),
        *update_param(norm_params, norm_total, norm_moment, norm_average, norm_rate),
        *updated(w_qkv, qkv_grad, qkv_moment, qkv_average),
        *updated(w_out, out_grad, out_moment, out_average),
        *updated(w_up, up_grad, up_moment, up_average),
        *updated(w_down, down_grad, down_moment, down_average),
    )


def solution(mesh):
    slots = P(None, None, ("seq", "mdl"), None)
    wide = P("seq", None, "mdl")
    flat = P("seq", "mdl")
    return jax.shard_map(
        per_device,
        mesh=mesh,
        in_specs=(
            *(slots, P(), slots, P(), wide, flat, flat, flat),
            *(P(), P(), wide, wide, flat, flat, flat, flat, flat, flat),
        ),
        out_specs=(
            *(slots, slots, P(), P(), P(), P()),
            *(wide,) * 4,
            *(flat,) * 12,
        ),
        check_vma=False,
    )
```

```python
import functools
import itertools

import jax
import jax.numpy as jnp
from jax import lax
from jax.experimental import pallas as pl
from jax.experimental.pallas import tpu as pltpu
from jax.sharding import PartitionSpec as P

HD = 64
LANES = 128

EPSILON = 1e-05
HALF_ROOT = 0.7071067811865476
INV_ROOT_TWO_PI = 0.3989422804014327
BF16 = jnp.bfloat16
F32 = jnp.float32


def norm_forward(values, gain, shift):
    row_mean = jnp.mean(values, -1, keepdims=True)
    centred = values - row_mean
    inv_std = lax.rsqrt(jnp.mean(centred * centred, -1, keepdims=True) + EPSILON)
    normed = centred * inv_std
    return (normed * gain + shift, normed, inv_std)


def norm_backward(upstream, normed, inv_std, gain):
    scaled = upstream * gain
    return inv_std * (
        scaled
        - jnp.mean(scaled, -1, keepdims=True)
        - normed * jnp.mean(scaled * normed, -1, keepdims=True)
    )


def update_param(weight, grad, moment, average, rate):
    new_moment = 0.5 * moment + grad
    new_weight = weight - rate * (grad + 0.5 * new_moment)
    new_average = 0.5 * average + 0.5 * new_weight
    return (new_moment, new_average, new_weight, new_weight.astype(BF16))


def dot(a, b, dims):
    return lax.dot_general(a, b, (dims, ((), ())), preferred_element_type=F32)


def tied(value, earlier):
    return lax.optimization_barrier((value, earlier))


def whole_sum(value, axes):
    for axis in axes:
        count = lax.axis_size(axis)
        step = 1
        while step < count:
            value = value + lax.ppermute(value, axis, [(i, i ^ step) for i in range(count)])
            step *= 2
    return value


def score_blocks(keys, queries, kpos, first, last, start, size):
    diag = dot(keys[start : start + size], queries, ((1,), (1,)))
    pos = kpos[start : start + size]
    diag = jnp.where((pos >= first) & (pos <= last), diag, -1e30)
    if not start:
        return [diag]
    ahead = dot(keys[:start], queries, ((1,), (1,)))
    return [jnp.where(kpos[:start] >= first, ahead, -1e30), diag]


def attend_kernel(own_ref, kpos_ref, meta_ref, q_ref, k_ref, v_ref, o_ref, lse_ref, *, size, factor):
    slots = kpos_ref.shape[0]
    count, short = q_ref.shape[1:3]
    per = count * short
    own = own_ref[0]
    heads = LANES // HD
    keys = k_ref[...].reshape(slots, LANES)
    values = v_ref[...].reshape(slots, LANES)
    kpos = kpos_ref[...]
    for start in range(0, slots, size):
        span = pl.ds(start // per, size // per)
        queries = q_ref[span].reshape(size, LANES) * factor
        first = meta_ref[0:1, start : start + size]
        last = meta_ref[1:2, start : start + size]
        outs = []
        for head in range(heads):
            cols = slice(head * HD, (head + 1) * HD)
            blocks = score_blocks(keys[:, cols], queries[:, cols], kpos, first, last, start, size)
            top = functools.reduce(jnp.maximum, [jnp.max(b, 0, keepdims=True) for b in blocks])
            blocks = [jnp.exp(b - top) for b in blocks]
            total = functools.reduce(jnp.add, [jnp.sum(b, 0, keepdims=True) for b in blocks])
            lse_ref[head : head + 1, start : start + size] = top + jnp.log(total)
            inverse = 1.0 / total
            out = None
            offset = 0
            for b in blocks:
                rows = slice(offset, offset + b.shape[0])
                offset += b.shape[0]
                term = dot(values[rows, cols], (b * inverse).astype(BF16), ((0,), (0,)))
                out = term if out is None else out + term
            outs.append(out)
        merged = jnp.concatenate(outs, 0).T.astype(BF16)
        for j in range(count):
            place = lax.rem(own + (count - j), count)
            for k in range(size // per):
                rows = slice(k * per + j * short, k * per + (j + 1) * short)
                o_ref[start // per + k, place] = merged[rows]


def attend_back_kernel(
    own_ref, kpos_ref, meta_ref, lse_ref, q_ref, k_ref, v_ref, g_ref, out_ref, dk_acc, dv_acc, *, size, factor
):
    slots = kpos_ref.shape[0]
    count, short = q_ref.shape[1:3]
    per = count * short
    own = own_ref[0]
    heads = LANES // HD
    keys = k_ref[...].reshape(slots, LANES)
    values = v_ref[...].reshape(slots, LANES)
    kpos = kpos_ref[...]
    dk_acc[...] = jnp.zeros_like(dk_acc)
    dv_acc[...] = jnp.zeros_like(dv_acc)
    for start in range(0, slots, size):
        span = pl.ds(start // per, size // per)
        queries = q_ref[span].reshape(size, LANES) * factor
        upstream = jnp.concatenate(
            [
                g_ref[start // per + k, lax.rem(own + (count - j), count)]
                for k in range(size // per)
                for j in range(count)
            ],
            0,
        )
        first = meta_ref[0:1, start : start + size]
        last = meta_ref[1:2, start : start + size]
        dqs, dks, dvs = [], [], []
        for head in range(heads):
            cols = slice(head * HD, (head + 1) * HD)
            blocks = score_blocks(keys[:, cols], queries[:, cols], kpos, first, last, start, size)
            lse = lse_ref[head : head + 1, start : start + size]
            probs = [jnp.exp(b - lse) for b in blocks]
            edges = [0] + ([start] if start else []) + [start + size]
            rows = [slice(a, b) for a, b in zip(edges[:-1], edges[1:])]
            back = [dot(values[r, cols], upstream[:, cols], ((1,), (1,))) for r in rows]
            terms = [p * b for p, b in zip(probs, back)]
            weighted = functools.reduce(jnp.add, [jnp.sum(t, 0, keepdims=True) for t in terms])
            score_back = [(t - p * weighted).astype(BF16) for t, p in zip(terms, probs)]
            dks.append([dot(s, queries[:, cols], ((1,), (0,))) for s in score_back])
            dvs.append([dot(p.astype(BF16), upstream[:, cols], ((1,), (0,))) for p in probs])
            dq = [dot(keys[r, cols], s, ((0,), (0,))) for r, s in zip(rows, score_back)]
            dqs.append(functools.reduce(jnp.add, dq) * factor)
        merged = jnp.concatenate(dqs, 0).T.astype(BF16)
        out_ref[span, 0] = merged.reshape(size // per, *out_ref.shape[2:])
        for i, r in enumerate(rows):
            dk_acc[r] += jnp.concatenate([d[i] for d in dks], 1)
            dv_acc[r] += jnp.concatenate([d[i] for d in dvs], 1)
    shape = (out_ref.shape[0], *out_ref.shape[2:])
    out_ref[:, 1] = dk_acc[...].astype(BF16).reshape(shape)
    out_ref[:, 2] = dv_acc[...].astype(BF16).reshape(shape)


def kind_spec(shape, kind):
    seq, _, _, blocks, short, lanes = shape
    return pl.BlockSpec(
        (seq, None, None, blocks, short, lanes), lambda r, kind=kind: (0, kind, r, 0, 0, 0)
    )


def attention(own, qkv, kpos, meta, size):
    seq, _, units, blocks, short, lanes = qkv.shape
    slots = kpos.shape[0]
    heads = LANES // HD
    work = units * heads * slots * slots * 5 // 8
    return pl.pallas_call(
        functools.partial(attend_kernel, size=size, factor=HD**-0.5),
        grid=(units,),
        in_specs=[
            pl.BlockSpec(memory_space=pltpu.SMEM),
            pl.BlockSpec((slots, 1), lambda r: (0, 0)),
            pl.BlockSpec((None, 2, slots), lambda r: (r, 0, 0)),
            *(kind_spec(qkv.shape, kind) for kind in range(3)),
        ],
        out_specs=[
            pl.BlockSpec((seq, blocks, None, short, lanes), lambda r: (0, 0, r, 0, 0)),
            pl.BlockSpec((None, heads, slots), lambda r: (r, 0, 0)),
        ],
        out_shape=[
            jax.ShapeDtypeStruct((seq, blocks, units, short, lanes), BF16),
            jax.ShapeDtypeStruct((units, heads, slots), F32),
        ],
        compiler_params=pltpu.CompilerParams(vmem_limit_bytes=48 << 20),
        cost_estimate=pl.CostEstimate(
            flops=work * HD * 4 * 4, bytes_accessed=units * slots * LANES * 8, transcendentals=work
        ),
        name="attend",
    )(own, kpos, meta, qkv, qkv, qkv)


def attention_back(own, qkv, upstream, lse, kpos, meta, size):
    seq, _, units, blocks, short, lanes = qkv.shape
    slots = kpos.shape[0]
    heads = LANES // HD
    work = units * heads * slots * slots * 5 // 8
    return pl.pallas_call(
        functools.partial(attend_back_kernel, size=size, factor=HD**-0.5),
        grid=(units,),
        in_specs=[
            pl.BlockSpec(memory_space=pltpu.SMEM),
            pl.BlockSpec((slots, 1), lambda r: (0, 0)),
            pl.BlockSpec((None, 2, slots), lambda r: (r, 0, 0)),
            pl.BlockSpec((None, heads, slots), lambda r: (r, 0, 0)),
            *(kind_spec(qkv.shape, kind) for kind in range(3)),
            pl.BlockSpec((seq, blocks, None, short, lanes), lambda r: (0, 0, r, 0, 0)),
        ],
        out_specs=pl.BlockSpec((seq, 3, None, blocks, short, lanes), lambda r: (0, 0, r, 0, 0, 0)),
        out_shape=jax.ShapeDtypeStruct(qkv.shape, BF16),
        scratch_shapes=[pltpu.VMEM((slots, LANES), F32), pltpu.VMEM((slots, LANES), F32)],
        compiler_params=pltpu.CompilerParams(vmem_limit_bytes=48 << 20),
        cost_estimate=pl.CostEstimate(
            flops=work * HD * 10 * 4, bytes_accessed=units * slots * LANES * 16, transcendentals=work
        ),
        name="attend_back",
    )(own, kpos, meta, lse, qkv, qkv, qkv, upstream)


def place_kernel(*refs, moves):
    *sources, target = refs
    for which, source, destination in moves:
        target[destination] = sources[which][source]


def placed(values, shape, moves, name):
    size = 2 * values[0].size * len(values)
    return pl.pallas_call(
        functools.partial(place_kernel, moves=moves),
        in_specs=[pl.BlockSpec(memory_space=pltpu.VMEM)] * len(values),
        out_specs=pl.BlockSpec(memory_space=pltpu.VMEM),
        out_shape=jax.ShapeDtypeStruct(shape, BF16),
        compiler_params=pltpu.CompilerParams(vmem_limit_bytes=32 << 20),
        cost_estimate=pl.CostEstimate(flops=0, bytes_accessed=2 * size, transcendentals=0),
        name=name,
    )(*values)


def per_device(
    layer_in,
    doc_ids,
    cotangent,
    norm_params,
    w_qkv,
    w_out,
    w_up,
    w_down,
    norm_moment,
    norm_average,
    qkv_moment,
    qkv_average,
    out_moment,
    out_average,
    up_moment,
    up_average,
    down_moment,
    down_average,
):
    mdl_count = lax.axis_size("mdl")
    seq_count = lax.axis_size("seq")
    micro, rows, short, width = layer_in.shape
    slots = doc_ids.shape[2]
    slot_dev = short * mdl_count
    embed = w_qkv.shape[2]
    pairs = embed // LANES
    groups = seq_count // pairs
    units = micro * rows // groups
    tokens = micro * rows * short
    size = slot_dev * max(1, 256 // slot_dev)
    seq_index = lax.axis_index("seq")
    mdl_index = lax.axis_index("mdl")

    behind = (mdl_index - jnp.arange(mdl_count, dtype=jnp.int32)) % mdl_count
    order = (
        jnp.arange(seq_count, dtype=jnp.int32)[:, None, None] * slot_dev
        + behind[None, :, None] * short
        + jnp.arange(short, dtype=jnp.int32)
    ).reshape(slots)
    docs = doc_ids.reshape(groups, units, slots)
    docs = lax.dynamic_index_in_dim(docs, seq_index % groups, 0, False)
    first = jnp.sum(
        ((docs[..., None, :] >= 0) & (docs[..., None, :] < docs[..., :, None])).astype(jnp.int32), -1
    )
    first = jnp.where(docs >= 0, first, jnp.arange(slots, dtype=jnp.int32))
    first = first.reshape(units, seq_count, mdl_count, short)
    first = jnp.stack(
        [lax.dynamic_index_in_dim(first, behind[j], 2, False) for j in range(mdl_count)], 2
    ).reshape(units, slots)
    meta = jnp.stack([first, jnp.broadcast_to(order, first.shape)], 1)
    kpos = order[:, None]
    own = mdl_index.reshape(1).astype(jnp.int32)

    def exchange(value):
        return lax.all_to_all(value, "seq", 0, 0, tiled=True)

    def exchange_all(value):
        shape = (seq_count * mdl_count, units, short, LANES)
        return lax.all_to_all(value.reshape(shape), ("seq", "mdl"), 0, 0, tiled=True)

    def row_tile(group, unit):
        start = (group * units + unit) * short
        return slice(start, start + short)

    def column_tile(index, pair):
        start = (index * pairs + pair) * LANES
        return slice(start, start + LANES)

    spots = list(itertools.product(range(groups), range(units), range(pairs)))

    def own_heads(value):
        moves = [
            (0, ((p * groups + g) * mdl_count + m, u), (row_tile(g, u), column_tile(m, p)))
            for g, u, p in spots
            for m in range(mdl_count)
        ]
        return placed([value], (tokens, mdl_count * embed), moves, "own_heads")

    def own_units(value):
        moves = [
            (0, (row_tile(g, u), column_tile(m, p)), ((p * groups + g) * mdl_count + m, u))
            for g, u, p in spots
            for m in range(mdl_count)
        ]
        shape = (seq_count * mdl_count, units, short, LANES)
        return placed([value], shape, moves, "own_units")

    def to_units(values):
        moves = [
            (j, (row_tile(g, u), column_tile(k, p)), (p * groups + g, k, u, j))
            for g, u, p in spots
            for k in range(3)
            for j in range(mdl_count)
        ]
        shape = (seq_count, 3, units, mdl_count, short, LANES)
        return placed(values, shape, moves, "to_units")

    def from_units(value):
        moves = [
            (0, (p * groups + g, k, u, j), (j, row_tile(g, u), column_tile(k, p)))
            for g, u, p in spots
            for k in range(3)
            for j in range(mdl_count)
        ]
        return placed([value], (mdl_count, tokens, 3 * embed), moves, "from_units")

    ring = [(i, (i + 1) % mdl_count) for i in range(mdl_count)]
    members = range(mdl_count)

    def pass_on(value):
        return lax.ppermute(value, "mdl", ring)

    held = {}

    def behind(value, *names):
        for name in names:
            value, held[name] = tied(value, held[name])
        return value

    def ring_gather(value, gates=()):
        parts = [value]
        for j in members[1:]:
            ahead = parts[-1]
            if j <= len(gates) and gates[j - 1]:
                ahead = behind(ahead, gates[j - 1])
            parts.append(pass_on(ahead))
        return parts

    def ring_terms(parts):
        carried = None
        for j in members[1:]:
            term = parts[j] if carried is None else parts[j] + carried.astype(F32)
            carried = yield term.astype(BF16)

    def ring_scatter(parts):
        terms = ring_terms(parts)
        term = next(terms)
        while True:
            carried = pass_on(term)
            try:
                term = terms.send(carried)
            except StopIteration:
                return carried

    def spread(weight):
        return lax.all_gather(weight, "seq", axis=0, tiled=True)

    def by_member(parts):
        placed = []
        for k in members:
            turns = (mdl_index - k) % mdl_count
            value = parts[0]
            for j in members[1:]:
                value = jnp.where(turns == j, parts[j], value)
            placed.append(value)
        return jnp.concatenate(placed, 1)

    def grad(left, right):
        return dot(left, right, ((0,), (0,))).astype(BF16)

    chips = seq_count // 2
    cycle = [*range(0, chips, 2), *range(chips - 1, 0, -2)]
    swap = [(i, i ^ 1) for i in range(seq_count)]
    onward, blocks_behind = [], []
    for index in range(seq_count):
        place, way = cycle.index(index // 2), 1 - 2 * (index % 2)
        onward.append((index, 2 * cycle[(place + way) % chips] + index % 2))
        blocks_behind.append([cycle[(place - way * j) % chips] for j in range(chips)])
    blocks_behind = lax.dynamic_index_in_dim(
        jnp.array(blocks_behind, jnp.int32), seq_index, 0, False
    )
    core = seq_index % 2

    def shared(value):
        return lax.psum_scatter(value, "seq", scatter_dimension=0, tiled=True).astype(F32)

    def share(value):
        value = value.reshape(chips, 2, -1, value.shape[-1])
        other = lax.ppermute(lax.dynamic_index_in_dim(value, 1 - core, 1, False), "seq", swap)

        def term(j):
            block = blocks_behind[j]
            zero = jnp.zeros_like(block)
            mine = lax.dynamic_slice(
                value, (block, core, zero, zero), (1, 1, *value.shape[2:])
            ).reshape(value.shape[2:])
            return mine.astype(F32) + lax.dynamic_index_in_dim(other, block, 0, False).astype(F32)

        carried = lax.ppermute(term(1).astype(BF16), "seq", onward)
        for j in range(2, chips):
            carried = lax.ppermute((term(j) + carried.astype(F32)).astype(BF16), "seq", onward)
        return term(0) + carried.astype(F32)

    total_tokens = micro * rows * slots
    weight_rate = 0.02 * total_tokens ** (-0.5)
    norm_rate = 0.15 * total_tokens ** (-0.5)
    inputs = layer_in.reshape(tokens, width)
    upstream = cotangent.reshape(tokens, width)

    low_qkv = w_qkv.astype(BF16).reshape(-1, 3 * embed)
    normed, hat_one, inv_one = norm_forward(inputs, norm_params[0], norm_params[1])
    normed, low_qkv = tied(normed.astype(BF16), low_qkv)
    full_qkv = spread(low_qkv)
    rows_one = ring_gather(normed)
    low_out, (full_qkv, rows_one[1]) = tied(w_out.astype(BF16), (full_qkv, rows_one[1]))
    wide = lax.all_gather(low_out, "mdl", axis=1, tiled=True)
    wide, rows_one[-1] = tied(wide, rows_one[-1])
    full_out = spread(wide)
    units_in = to_units([dot(part, full_qkv, ((1,), (0,))).astype(BF16) for part in rows_one])
    low_up, units_in = tied(w_up.astype(BF16), units_in)
    full_up = spread(low_up)
    held["one"] = rows_one[-1]
    back = behind(upstream.astype(BF16), "one")
    rows_one[-1] = held["one"]
    rows_back = [back, pass_on(back)]
    qkv = exchange(units_in)
    for j in members[2:]:
        rows_back.append(pass_on(rows_back[-1]))
    qkv, rows_back[-2] = tied(qkv, rows_back[-2])
    rows_back[-1] = pass_on(rows_back[-2])

    heads, lse = attention(own, qkv, kpos, meta, size)
    low_down, held["lse"] = tied(w_down.astype(BF16), lse)
    full_down = spread(low_down)
    heads = exchange_all(heads)
    heads, (full_up, rows_back[-1]) = tied(heads, (full_up, rows_back[-1]))
    attended = own_heads(heads)
    middle = inputs + dot(attended, full_out, ((1,), (1,)))
    normed, hat_two, inv_two = norm_forward(middle, norm_params[2], norm_params[3])
    normed = normed.astype(BF16)

    rows_two = [normed]
    hidden, up_back, second = [None] * mdl_count, [None] * mdl_count, [None] * mdl_count

    def feed(j):
        up_proj = dot(rows_two[j], full_up, ((1,), (0,)))
        cdf = 0.5 * (1.0 + lax.erf(up_proj * HALF_ROOT))
        slope = cdf + up_proj * jnp.exp(-0.5 * up_proj * up_proj) * INV_ROOT_TWO_PI
        hidden[j] = (up_proj * cdf).astype(BF16)
        up_back[j] = (dot(rows_back[j], full_down, ((1,), (0,))) * slope).astype(BF16)
        second[j] = dot(up_back[j], full_up, ((1,), (1,)))

    for j in members[1:]:
        ahead = rows_two[-1]
        if j > 2:
            ahead, hidden[j - 2] = tied(ahead, hidden[j - 2])
            rows_two[-1] = ahead
        rows_two.append(pass_on(ahead))
        feed(j)
    feed(0)
    terms = ring_terms(second)
    term = next(terms)
    for j in members[2:]:
        carried = pass_on(term)
        term = terms.send(carried)
        if j == 2:
            rows_back[0], term = tied(rows_back[0], term)
    rows_two[0], term = tied(rows_two[0], term)
    second_sum = pass_on(term)
    down_part = grad(jnp.concatenate(rows_back, 0), jnp.concatenate(hidden, 0))
    up_part = grad(jnp.concatenate(rows_two, 0), jnp.concatenate(up_back, 0))
    second_sum, (down_part, up_part) = tied(second_sum, (down_part, up_part))
    held["down"] = shared(down_part)
    second_in = second[0] + second_sum.astype(F32)
    middle_grad = upstream + norm_backward(second_in, hat_two, inv_two, norm_params[2])
    middle_low = middle_grad.astype(BF16)

    attended_back = dot(middle_low, full_out, ((1,), (0,))).astype(BF16)
    hidden, attended_back = tied(hidden, attended_back)
    branch = [dot(value, full_down, ((1,), (1,))) for value in hidden]
    held["unit"] = exchange_all(own_units(attended_back))
    branch_terms = ring_terms(branch)
    held["unit"], branch[:] = tied(held["unit"], branch)
    carried = pass_on(behind(next(branch_terms), "unit"))
    out_part = grad(behind(middle_low, "unit"), attended)
    held["attg"] = attention_back(
        own,
        qkv,
        held["unit"].reshape(seq_count, mdl_count, units, short, LANES),
        held["lse"],
        kpos,
        meta,
        size,
    )
    for _ in members[2:-1]:
        carried = pass_on(branch_terms.send(behind(carried, "attg")))
    proj_back = from_units(exchange(held["attg"]))
    proj_back, (up_part, out_part) = tied(proj_back, (up_part, out_part))
    held["out"] = shared(out_part)
    first = [dot(proj_back[j], full_qkv, ((1,), (1,))) for j in members]
    first_terms = ring_terms(first)
    term = next(first_terms)
    (proj_back, up_part), term = tied((proj_back.reshape(-1, 3 * embed), up_part), term)
    held["up"] = shared(up_part)
    first_sum, first[:] = tied(pass_on(term), first)
    qkv_part = grad(jnp.concatenate(rows_one, 0), proj_back)
    term = first_terms.send(first_sum)
    for _ in members[3:]:
        term = first_terms.send(pass_on(term))
    qkv_part, term = tied(qkv_part, term)
    first_sum = pass_on(term)
    held["qkv_grad"] = share(qkv_part)
    columns = jnp.stack(jnp.split(held["out"].astype(BF16), mdl_count, 1))
    columns = lax.all_to_all(columns, "mdl", 0, 0, tiled=True)
    held["out_grad"] = jnp.sum(columns.astype(F32), 0)
    second_late, first[0] = tied((second_in, hat_two), first[0])
    second_sums = [jnp.sum(second_late[0] * second_late[1], 0), jnp.sum(second_late[0], 0)]
    held["sums"] = second_sums
    first_sum = behind(first_sum, "down", "sums")
    carried, first_sum = tied(carried, first_sum)
    carried = pass_on(branch_terms.send(carried))
    layer_out = middle + (branch[0] + carried.astype(F32))
    down_grad, up_grad = held["down"], held["up"]
    out_grad, qkv_grad = held["out_grad"], held["qkv_grad"]
    first_in = first[0] + first_sum.astype(F32)
    input_grad = middle_grad + norm_backward(first_in, hat_one, inv_one, norm_params[0])
    norm_sums = jnp.stack(
        [jnp.sum(first_in * hat_one, 0), jnp.sum(first_in, 0), *held["sums"]]
    )
    norm_sums, (qkv_grad, out_grad, layer_out) = tied(norm_sums, (qkv_grad, out_grad, layer_out))
    norm_total = whole_sum(norm_sums, ("mdl", "seq"))

    def updated(weight, total, moment, average):
        if weight.ndim == 2:
            return update_param(weight, total, moment, average, weight_rate)
        kinds = [value.swapaxes(0, 1) for value in (weight, moment, average)]
        total = jnp.stack(jnp.split(total, 3, 1))
        new = update_param(kinds[0], total, *kinds[1:], weight_rate)
        return [value.swapaxes(0, 1) for value in new]

    shape = layer_in.shape
    return (
        layer_out.reshape(shape),
        input_grad.reshape(shape),
        *update_param(norm_params, norm_total, norm_moment, norm_average, norm_rate),
        *updated(w_qkv, qkv_grad, qkv_moment, qkv_average),
        *updated(w_out, out_grad, out_moment, out_average),
        *updated(w_up, up_grad, up_moment, up_average),
        *updated(w_down, down_grad, down_moment, down_average),
    )


def solution(mesh):
    slots = P(None, None, ("seq", "mdl"), None)
    wide = P("seq", None, "mdl")
    flat = P("seq", "mdl")
    return jax.shard_map(
        per_device,
        mesh=mesh,
        in_specs=(
            *(slots, P(), slots, P(), wide, flat, flat, flat),
            *(P(), P(), wide, wide, flat, flat, flat, flat, flat, flat),
        ),
        out_specs=(
            *(slots, slots, P(), P(), P(), P()),
            *(wide,) * 4,
            *(flat,) * 12,
        ),
        check_vma=False,
    )
```
